32 devices in a mesh: facet: 8 (over z, y), col: 4 (over x, core).
Axes of the slice: x: 2, y: 2, z: 4, core: 2. Of those that a mesh axis runs over, the one named last changes fastest.
Arguments:
- prepared: bfloat16 [8, 2, 8192, 512], P('facet', None, None, 'col'), may hold values from -6 to 6
- sub_off: int32 [8, 4], P(None, 'col'), may hold values from 0 to 8191
- fac_off: int32 [8], replicated, may hold values from 0 to 511
- win_col: int32 [4, 128], replicated, may hold values from 0 to 255
- vis_weights: bfloat16 [8, 2, 512, 512], P('facet', None, None, 'col'), may hold values from -6 to 6
Outputs:
- facet_strips: bfloat16 [8, 2, 8192, 256], P('facet', None, 'col')
The draws below stay inside these ranges and needn't reach their ends.
All inputs are finite; a program needn't handle non-finite values.
Results may differ from the reference program's by a relative error of at most 0.0093.
Values may be sent and summed in bfloat16 or wider, within the bound.
A program may use at most 128 MiB of HBM per device.

```python
import math
import jax
import jax.numpy as jnp
from jax import lax

YF = 8192
XM = 128
XA = 512
CW = 128
FACETS = 8
NSUB = 8
OC = 256
N_COL = 4


def touch_ends(drawn, key, smallest, top_value):
    spot = [jax.random.randint(jax.random.fold_in(key, axis), (), 0, length) for axis, length in enumerate(drawn.shape)]
    main_axis = drawn.shape.index(max(drawn.shape))
    neighbour = spot[:main_axis] + [(spot[main_axis] + 1) % drawn.shape[main_axis]] + spot[main_axis + 1:]
    return drawn.at[tuple(spot)].set(smallest).at[tuple(neighbour)].set(top_value)


def levels(key, extent, pieces, smallest, high):
    loudness = 1.0
    for dim, blocks in pieces:
        steps = jax.random.uniform(jax.random.fold_in(jax.random.fold_in(key, 6), dim), (blocks,), jnp.float32, smallest / len(pieces), high / len(pieces))
        loudness = loudness * jnp.repeat(jnp.exp(steps), extent[dim] // blocks).reshape((-1,) + (1,) * (len(extent) - 1 - dim))
    return loudness


def centred(rng, dims, spread, reach, shards=(), held_as=jnp.bfloat16):
    values = jax.random.normal(rng, dims, jnp.float32) * spread
    if len(shards) > 0:
        values = levels(rng, dims, shards, -0.22, 0.18) * values
    return jnp.clip(values, min=-reach, max=reach).astype(held_as)


def setup_inputs(seed: int = 0) -> dict:
    splits = jax.random.split(jax.random.key(seed), 6)
    prepared = centred(splits[0], (FACETS, 2, YF, CW * N_COL), 1.0, 6.0, ((0, 8), (3, 4)))
    sub_off = touch_ends(jax.random.randint(splits[1], (NSUB, N_COL), 0, YF), jax.random.fold_in(splits[1], 1), 0, YF - 1).astype(jnp.int32)
    fac_off = touch_ends(jax.random.randint(splits[2], (FACETS,), 0, XA), jax.random.fold_in(splits[2], 1), 0, XA - 1).astype(jnp.int32)
    win_col = touch_ends(jax.random.randint(splits[3], (N_COL, CW), 0, OC), jax.random.fold_in(splits[3], 1), 0, OC - 1).astype(jnp.int32)
    vis_weights = centred(splits[4], (NSUB, 2, XA, CW * N_COL), 1.0, 6.0, ((0, 8), (3, 4)))
    return {"prepared": prepared, "sub_off": sub_off, "fac_off": fac_off, "win_col": win_col, "vis_weights": vis_weights}


def taper_curve(length):
    position = (jnp.arange(length, dtype=jnp.float32) + 0.5) / length
    return 0.3 + 0.7 * jnp.sin(math.pi * position) ** 2

def phases(row_ids, col_ids, length, sign_factor, scaling):
    products = row_ids[:, None] * col_ids[None, :] % length
    angles = 2.0 * math.pi / length * products.astype(jnp.float32)
    return (jnp.cos(angles) * scaling, sign_factor * jnp.sin(angles) * scaling)

def complex_block(real_part, imag_part):
    upper_rows = jnp.concatenate([real_part, -imag_part], axis=1)
    lower_rows = jnp.concatenate([imag_part, real_part], axis=1)
    return jnp.concatenate([upper_rows, lower_rows], axis=0).astype(jnp.bfloat16)

def small_tables(length):
    positions = jnp.arange(length, dtype=jnp.int32)
    taper_vals = taper_curve(length)
    fwd_re, fwd_im = phases(positions, positions, length, -1.0, 1.0 / math.sqrt(length))
    back_re, back_im = phases(positions, positions, length, 1.0, 1.0 / math.sqrt(length))
    forward = complex_block(fwd_re * taper_vals[None, :], fwd_im * taper_vals[None, :])
    backward = complex_block(back_re * taper_vals[:, None], back_im * taper_vals[:, None])
    return (forward, backward)

def grid_tables(length, facet_count, contrib_len):
    positions = jnp.arange(length, dtype=jnp.int32)
    fwd_re, fwd_im = phases(positions, positions, length, -1.0, 1.0 / math.sqrt(facet_count * contrib_len))
    back_re, back_im = phases(positions, positions, length, 1.0, 1.0 / math.sqrt(length))
    return (complex_block(fwd_re, fwd_im), complex_block(back_re, back_im))

def finish_map(columns, out_cols):
    frequency = jnp.arange(out_cols, dtype=jnp.int32)
    products = columns[:, None] * frequency[None, :] % out_cols
    angles = 2.0 * math.pi / out_cols * products.astype(jnp.float32)
    scaling = 1.0 / math.sqrt(2 * out_cols)
    real_part = jnp.cos(angles) * scaling
    imag_part = jnp.sin(angles) * scaling
    from_real = jnp.concatenate([real_part, imag_part], axis=1)
    from_imag = jnp.concatenate([-imag_part, real_part], axis=1)
    return jnp.stack([from_real, from_imag], axis=0).astype(jnp.bfloat16)

def apply_weights(spectrum, weights):
    spec_re = spectrum[..., 0, :, :]
    spec_im = spectrum[..., 1, :, :]
    weight_re = weights[..., 0, :, :].astype(jnp.float32)
    weight_im = weights[..., 1, :, :].astype(jnp.float32)
    joined = jnp.stack([weight_re * spec_re - weight_im * spec_im, weight_re * spec_im + weight_im * spec_re], axis=-3)
    return joined.astype(jnp.bfloat16)

def reference(prepared, sub_off, fac_off, win_col, vis_weights):
    forward_small, backward_small = small_tables(XM)
    forward_grid, backward_grid = grid_tables(XA, FACETS, XM)
    window_pos = jnp.arange(XM, dtype=jnp.int32)
    dest_rows = ((fac_off[:, None] + window_pos[None, :]) % XA).reshape(-1)

    def one_column(column):
        strips = lax.dynamic_slice_in_dim(prepared, column * CW, CW, 3)
        offsets = lax.dynamic_index_in_dim(sub_off, column, 1, keepdims=False)
        weights = lax.dynamic_slice_in_dim(vis_weights, column * CW, CW, 3)

        def one_subgrid(subgrid_item):
            first_row, weight_block = subgrid_item
            src_rows = (first_row + window_pos) % YF
            picked = strips[:, :, src_rows].reshape(FACETS, 2 * XM, CW)
            contrib = jnp.einsum('ab,fbc->fac', forward_small.astype(jnp.float32), picked.astype(jnp.float32)).astype(jnp.bfloat16)
            flat_rows = contrib.reshape(FACETS, 2, XM, CW).transpose(1, 0, 2, 3).reshape(2, FACETS * XM, CW).astype(jnp.float32)
            assembled = jnp.zeros((2, XA, CW), jnp.float32).at[:, dest_rows].add(flat_rows).astype(jnp.bfloat16)
            spectrum = jnp.dot(forward_grid, assembled.reshape(2 * XA, CW), preferred_element_type=jnp.float32).reshape(2, XA, CW)
            weighted = apply_weights(spectrum, weight_block)
            grid_image = jnp.dot(backward_grid, weighted.reshape(2 * XA, CW), preferred_element_type=jnp.float32).astype(jnp.bfloat16).reshape(2, XA, CW)
            return grid_image[:, dest_rows].reshape(2, FACETS, XM, CW).transpose(1, 0, 2, 3)
        return lax.map(one_subgrid, (offsets, weights))
    returned = lax.map(one_column, jnp.arange(N_COL, dtype=jnp.int32))
    all_rows = (sub_off[:, :, None] + window_pos[None, None, :]) % YF

    def one_facet(facet_index):
        summed = jnp.zeros((YF, 2 * OC), jnp.float32)
        for column in range(N_COL):
            back_part = returned[column, :, facet_index].reshape(NSUB, 2 * XM, CW)
            returned_terms = jnp.einsum('ab,sbc->sac', backward_small.astype(jnp.float32), back_part.astype(jnp.float32))
            returned_terms = returned_terms.reshape(NSUB, 2, XM, CW).transpose(1, 0, 2, 3).reshape(2, NSUB * XM, CW)
            accum = jnp.zeros((2, YF, CW), jnp.float32).at[:, all_rows[:, column].reshape(-1)].add(returned_terms)
            strip_sum = accum.astype(jnp.bfloat16)
            summed = summed + jnp.einsum('pyk,pkm->ym', strip_sum.astype(jnp.float32), finish_map(win_col[column], OC).astype(jnp.float32))
        return summed.astype(jnp.bfloat16).reshape(YF, 2, OC).transpose(1, 0, 2)
    return lax.map(one_facet, jnp.arange(FACETS, dtype=jnp.int32))
```

```python
import functools
import math

import jax
import jax.numpy as jnp
import numpy as np
from jax import lax
from jax.experimental import pallas as pl
from jax.experimental.pallas import tpu as pltpu
from jax.sharding import PartitionSpec as P

XM = 128
ALIGN = 16
CHUNKS = 8
OUT_CHUNKS = 8
VALUES_LIMIT = 16 * 2**20
VMEM_LIMIT = 40 * 2**20
MESH = pl.DeviceIdType.MESH
F32 = jnp.float32
BF16 = jnp.bfloat16


def dft(length, sign, scaling):
    ids = np.arange(length)
    angles = 2.0 * np.pi / length * (ids[:, None] * ids[None, :] % length)
    return np.cos(angles) * scaling, sign * np.sin(angles) * scaling


def stacked(real_part, imag_part, axis):
    return np.concatenate([real_part, imag_part], axis=axis).astype(jnp.bfloat16)


def window_tables(length):
    taper = 0.3 + 0.7 * np.sin(np.pi * (np.arange(length) + 0.5) / length) ** 2
    scaling = 1.0 / math.sqrt(length)
    fwd_re, fwd_im = dft(length, -1.0, scaling)
    back_re, back_im = dft(length, 1.0, scaling)
    forward = stacked(fwd_re * taper[None, :], fwd_im * taper[None, :], 0)
    backward = stacked(back_re * taper[:, None], back_im * taper[:, None], 1)
    return forward, backward


def mm(a, b):
    return jnp.dot(a, b, preferred_element_type=F32)


def iota(shape, dim):
    return lax.broadcasted_iota(jnp.int32, shape, dim)


def one_hot(hit):
    return jnp.where(hit, 1.0, 0.0).astype(BF16)


def exchange_kernel(
    nf, ncol, near, early, starts_in, fac_in, prep, wts, fwd_in, bwd_in, win_in, fmap, qtab,
    terms, values, maps, starts_out,
    starts, fac, fwd, bwd, win, pv, qv, wv, send1, recv1, acc, grid, send2, ctab, svec, sall, fv, wdup,
    ld, s1, r1, s2, sd, sx, sp, rt, ss, rs,
):
    me = lax.axis_index("facet")
    c = lax.axis_index("col")
    nx = ncol // 2
    xq, core = lax.div(c, 2), lax.rem(c, 2)
    partner = xq * 2 + 1 - core
    pow2 = nf & (nf - 1) == 0
    blocks = prep.shape[1]
    xa, width = wts.shape[1:]
    half = width // 2
    oc = fmap.shape[0]
    chunks = CHUNKS
    deep = nf <= 8
    step = blocks // chunks

    def peer(i):
        if not pow2:
            return lax.rem(me + i, nf)
        out, b = 0, 1
        while b < nf:
            mb, ib = lax.rem(lax.div(me, b), 2), lax.rem(lax.div(i, b), 2)
            out = out + b * (mb + ib - 2 * mb * ib)
            b *= 2
        return out

    def source(i):
        return peer(i) if pow2 else lax.rem(me + nf - i, nf)

    def across(q):
        return lax.rem(xq + q, nx) * 2 + core

    barrier = pltpu.get_barrier_semaphore()

    @pl.loop(1, nf)
    def _(i):
        pl.semaphore_signal(barrier, inc=1, device_id={"facet": peer(i)}, device_id_type=MESH)

    for i in range(1, ncol):
        pl.semaphore_signal(
            barrier, inc=1, device_id={"col": lax.rem(c + i, ncol)}, device_id_type=MESH
        )

    @pl.loop(1, near)
    def _(i):
        for q in range(1, nx):
            pl.semaphore_signal(
                barrier, inc=1, device_id={"facet": peer(i), "col": across(q)}, device_id_type=MESH
            )

    loads = [
        pltpu.make_async_copy(
            prep.at[:, pl.ds(k * step, step)], pv.at[:, pl.ds(k * step, step)], ld.at[k]
        )
        for k in range(chunks)
    ]
    small = [(starts_in, starts), (fac_in, fac), (fwd_in, fwd)]
    later = [(win_in, win), (fmap, fv), (bwd_in, bwd), (wts, wv), (qtab, qv)]
    small = [pltpu.make_async_copy(*pair, ld.at[chunks + k]) for k, pair in enumerate(small)]
    later = [pltpu.make_async_copy(*pair, ld.at[chunks + 3 + k]) for k, pair in enumerate(later)]
    for copy in small + loads + later:
        copy.start()
    win_load, f_load, b_load, w_load, q_load = later
    for copy in small:
        copy.wait()

    lane = iota(svec.shape, 1)
    row = jnp.zeros(svec.shape, jnp.int32)
    svec[...] = lax.fori_loop(0, nf, lambda j, v: jnp.where(lane == j, starts[j], v), row)

    def remote(src, dst, send, recv, **where):
        return pltpu.make_async_remote_copy(
            src_ref=src, dst_ref=dst, send_sem=send, recv_sem=recv,
            device_id=where, device_id_type=MESH,
        )

    def send_first(h, j):
        return remote(send1.at[h, j], recv1.at[h, me], s1.at[h, j], r1.at[h, me], facet=j)

    def recv_first(h, j):
        return remote(send1.at[h, j], recv1.at[h, j], s1.at[h, j], r1.at[h, j], facet=j)

    def send_second(h, j):
        return remote(send2.at[h, j], terms.at[c, me, h], s2.at[h, j], rt.at[c, me, h], facet=j)

    def send_direct(h, j, q):
        return remote(
            send2.at[h, j], terms.at[c, me, h], sd.at[q, j, h], rt.at[c, me, h],
            facet=j, col=across(q),
        )

    def arrival(cc, j, h):
        return remote(send2.at[h, j], terms.at[cc, j, h], s2.at[h, j], rt.at[cc, j, h], facet=j)

    def forward_x(src, j, h, q):
        return remote(
            src, terms.at[c, j, h], sx.at[q, j, h], rt.at[c, j, h], col=across(q)
        )

    def forward_partner(src, cc, j, h):
        return remote(src, terms.at[cc, j, h], sp.at[cc, j, h], rt.at[cc, j, h], col=partner)

    row_d = iota((XM, 2 * XM), 1) - iota((XM, 2 * XM), 0)
    fwd_table = fwd[...]

    def contribution(j, dst):
        start = starts[j]
        block = lax.div(start, XM)
        shift = lax.rem(start, XM)
        above = lax.rem(block + 1, blocks)
        top = jnp.concatenate([pv[0, block], pv[1, block]], axis=1)
        low = jnp.concatenate([pv[0, above], pv[1, above]], axis=1)
        picked = mm(one_hot(row_d == shift), jnp.concatenate([top, low], axis=0))
        prod = mm(fwd_table, picked.astype(BF16))
        re = prod[:XM, :width] - prod[XM:, width:]
        im = prod[:XM, width:] + prod[XM:, :width]
        first = iota(re.shape, 1) < half
        dst[0, j] = jnp.where(first, re, pltpu.roll(im, half, 1)).astype(BF16)
        dst[1, j] = jnp.where(first, pltpu.roll(re, half, 1), im).astype(BF16)

    def window_maps():
        win_load.wait()
        f_load.wait()
        fm = fv[...]
        col_n = iota((oc, width), 0)
        for k in range(ncol):
            m = lax.dot_general(
                one_hot(col_n == win[k : k + 1, :]), fm, (((0,), (0,)), ((), ())),
                preferred_element_type=F32,
            ).astype(BF16)
            m_re, m_im = m[:, :oc], m[:, oc:]
            upper = jnp.concatenate([m_re, m_im], axis=1)
            lower = jnp.concatenate([-m_im, m_re], axis=1)
            maps[k] = jnp.concatenate(
                [upper[:half], lower[:half], upper[half:], lower[half:]], axis=0
            )

    for copy in loads:
        copy.wait()
    pl.semaphore_wait(barrier, nf - 1 + ncol - 1 + (near - 1) * (nx - 1))

    @pl.loop(1, nf, unroll=deep)
    def _(i):
        j = peer(nf - i)
        contribution(j, send1)
        send_first(0, j).start()

    @pl.loop(1, nf)
    def _(i):
        send_first(1, peer(nf - i)).start()

    contribution(me, recv1)

    start_sends = []
    for i in range(1, ncol):
        to = lax.rem(c + i, ncol)
        start_sends.append(remote(svec, sall.at[c], ss.at[i], rs.at[c], col=to))
        start_sends[-1].start()
    sall[c] = svec[...]
    window_maps()

    b_load.wait()
    turn_d = iota((XM, XM), 0) - iota((XM, XM), 1)
    turn_by = lax.rem(starts[me], ALIGN)
    turn = (turn_d == turn_by) | (turn_d == turn_by - XM)
    turned = mm(one_hot(turn), bwd[...]).astype(BF16)
    turned = jnp.concatenate([turned[:, :XM], turned[:, XM:]], axis=0)
    back_d = iota((XM, xa), 1) - iota((XM, xa), 0)

    @pl.loop(0, nf, unroll=deep)
    def _(j):
        hit = (back_d == fac[j]) | (back_d == fac[j] - xa)
        ctab[j] = mm(turned, one_hot(hit)).astype(BF16)

    w_load.wait()
    near_lane = iota((xa, width), 1) < half
    for p in range(2):
        w = wv[p].astype(F32)
        swapped = pltpu.roll(w, half, 1)
        wdup[0, p] = jnp.where(near_lane, w, swapped)
        wdup[1, p] = jnp.where(near_lane, swapped, w)

    grid_d = iota((xa, XM), 0) - iota((xa, XM), 1)

    def place(h, j):
        hit = (grid_d == fac[j]) | (grid_d == fac[j] - xa)
        return mm(one_hot(hit), recv1[h, j])

    def twist(prod, conj):
        n = prod.shape[0] // 2
        crossed = pltpu.roll(prod[n:], half, 1)
        first = iota(crossed.shape, 1) < half
        minus = jnp.logical_not(first) if conj else first
        return prod[:n] + jnp.where(minus, -crossed, crossed)

    q_load.wait()
    own_copies = []
    for h in range(2):
        acc[...] = place(h, me)

        @pl.loop(1, nf)
        def _(i):
            j = source(nf - i)
            recv_first(h, j).wait_recv()
            acc[...] += place(h, j)

        table = qv[...]
        spectrum = twist(mm(table, acc[...].astype(BF16)), False)
        crossed = wdup[h, 1] * pltpu.roll(spectrum, half, 1)
        weighted = wdup[h, 0] * spectrum + jnp.where(near_lane, -crossed, crossed)
        image = twist(mm(table, weighted.astype(BF16)), True)
        grid[...] = (image * image_gain(nf, xa)).astype(BF16)

        def back(j):
            return twist(mm(ctab[j], grid[...]), False).astype(BF16)

        send2[h, me] = back(me)
        copy = pltpu.make_async_copy(
            send2.at[h, me], terms.at[c, me, h], ld.at[chunks + 8 + h]
        )
        copy.start()
        own_copies.append(copy)
        for q in range(1, nx):
            forward_x(send2.at[h, me], me, h, q).start()
        forward_partner(send2.at[h, me], c, me, h).start()

        @pl.loop(1, near, unroll=deep)
        def _(i):
            j = peer(i)
            send2[h, j] = back(j)
            send_second(h, j).start()
            for q in range(1, nx):
                send_direct(h, j, q).start()

        @pl.loop(near, nf, unroll=deep)
        def _(i):
            j = peer(i)
            send2[h, j] = back(j)
            send_second(h, j).start()

    for copy in own_copies:
        copy.wait()
    for i in range(1, ncol):
        start_sends[i - 1].wait_send()
        frm = lax.rem(c + ncol - i, ncol)
        remote(svec, sall.at[frm], ss.at[i], rs.at[frm], col=frm).wait_recv()
    starts_copy = pltpu.make_async_copy(sall, starts_out, ld.at[chunks + 10])
    starts_copy.start()

    def relay_near(h):
        @pl.loop(1, near)
        def _(i):
            j = source(i)
            arrival(c, j, h).wait_recv()
            forward_partner(terms.at[c, j, h], c, j, h).start()

        @pl.loop(0, near)
        def _(i):
            relay_across(source(i), h)

    def relay_far(j, h):
        arrival(c, j, h).wait_recv()
        for q in range(1, nx):
            forward_x(terms.at[c, j, h], j, h, q).start()
        forward_partner(terms.at[c, j, h], c, j, h).start()

    def relay_across(j, h):
        for q in range(1, nx):
            cc = across(q)
            arrival(cc, j, h).wait_recv()
            forward_partner(terms.at[cc, j, h], cc, j, h).start()

    def from_partner(j, h):
        for q in range(nx):
            arrival(lax.rem(xq + q, nx) * 2 + 1 - core, j, h).wait_recv()

    @pl.loop(near, nf)
    def _(i):
        relay_far(source(i), 0)

    relay_near(0)
    relay_near(1)

    @pl.loop(near, nf)
    def _(i):
        relay_far(source(i), 1)
        relay_across(source(i), 0)

    @pl.loop(0, near)
    def _(i):
        j = source(i)
        from_partner(j, 0)
        from_partner(j, 1)
        if early:
            for k in range(ncol):
                values[k, i] = mm(jnp.concatenate([terms[k, j, 0], terms[k, j, 1]], axis=1), maps[k])

    @pl.loop(near, nf)
    def _(i):
        relay_across(source(i), 1)

    @pl.loop(near, nf)
    def _(i):
        from_partner(source(i), 0)
        from_partner(source(i), 1)

    starts_copy.wait()
    for h in range(2):
        @pl.loop(0, nf)
        def _(j):
            for q in range(nx):
                forward_partner(terms.at[c, j, h], across(q), j, h).wait_send()

        for q in range(1, nx):
            forward_x(send2.at[h, me], me, h, q).wait_send()

        @pl.loop(near, nf)
        def _(i):
            j = source(i)
            for q in range(1, nx):
                forward_x(terms.at[c, j, h], j, h, q).wait_send()

        @pl.loop(1, near)
        def _(i):
            for q in range(1, nx):
                send_direct(h, peer(i), q).wait_send()

        @pl.loop(1, nf)
        def _(i):
            send_first(h, peer(i)).wait_send()
            send_second(h, peer(i)).wait_send()


def image_gain(nf, xa):
    return math.sqrt(nf * XM) / math.sqrt(xa)


def finish_kernel(nf, ncol, near, early, starts_all, terms, values, maps, out, acc, stage, osem):
    me = lax.axis_index("facet")
    c = lax.axis_index("col")
    own_rows = out.shape[1]
    oc = out.shape[2]
    total = own_rows * ncol
    base = c * own_rows
    pow2 = nf & (nf - 1) == 0

    def source(i):
        if not pow2:
            return lax.rem(me + nf - i, nf)
        return jnp.bitwise_xor(me, i)

    acc[...] = jnp.zeros_like(acc)
    slot = iota((XM, 2 * oc), 0)
    edge = iota((ALIGN, 2 * oc), 0)

    def gather(first, last, value_of):
        @pl.loop(first * ncol, last * ncol)
        def _(t):
            i, cc = lax.div(t, ncol), lax.rem(t, ncol)
            j = source(i)
            rel = starts_all[cc, 0, j] - base + XM
            rel = jnp.where(rel < 0, rel + total, rel)
            rel = jnp.where(rel >= total, rel - total, rel)

            @pl.when(rel < own_rows + XM)
            def _():
                value = value_of(cc, i, j)
                turn = lax.rem(rel, ALIGN)
                low = pl.multiple_of(rel - turn, ALIGN)
                acc[pl.ds(low, XM), :] += jnp.where(slot >= turn, value, 0.0)
                acc[pl.ds(pl.multiple_of(low + XM, ALIGN), ALIGN), :] += jnp.where(
                    edge < turn, value[:ALIGN], 0.0
                )

    def mapped(cc, i, j):
        return mm(jnp.concatenate([terms[cc, j, 0], terms[cc, j, 1]], axis=1), maps[cc])

    split = near if early else 0
    if early:
        gather(0, split, lambda cc, i, j: values[cc, i])
    gather(split, nf, mapped)

    chunk = own_rows // OUT_CHUNKS
    copies = []
    for k in range(OUT_CHUNKS):
        rows = pl.ds(k * chunk, chunk)
        src = pl.ds(XM + k * chunk, chunk)
        stage[0, rows, :] = acc[src, :oc].astype(BF16)
        stage[1, rows, :] = acc[src, oc:].astype(BF16)
        copy = pltpu.make_async_copy(stage.at[:, rows, :], out.at[:, rows, :], osem.at[k])
        copy.start()
        copies.append(copy)
    for copy in copies:
        copy.wait()


def body(prepared, sub_off, fac_off, win_col, vis_weights):
    nf = fac_off.shape[0]
    ncol = lax.axis_size("col")
    facet_strip = prepared[0]
    facet_len, width = facet_strip.shape[1:]
    strip_blocks = facet_strip.reshape(2, facet_len // XM, XM, width)
    weights = vis_weights[0]
    xa = weights.shape[1]
    oc = width * ncol // 2
    own_rows = facet_len // ncol
    starts = sub_off[:, 0]
    lanes = -(-nf // 128) * 128
    near = nf // 2 if nf & (nf - 1) == 0 else 1
    early = ncol * near * XM * 2 * oc * 4 <= VALUES_LIMIT

    forward, backward = window_tables(XM)
    q_table = stacked(*dft(xa, -1.0, 1.0 / math.sqrt(nf * XM)), 0)
    out_map = stacked(*dft(oc, 1.0, 1.0 / math.sqrt(2 * oc)), 1)

    smem = pl.BlockSpec(memory_space=pltpu.SMEM)
    vmem = pl.BlockSpec(memory_space=pltpu.VMEM)
    hbm = pl.BlockSpec(memory_space=pl.ANY)
    dma = pltpu.SemaphoreType.DMA
    halves = pltpu.VMEM((2, nf, XM, width), BF16)
    operands = (
        starts, fac_off, strip_blocks, weights, jnp.asarray(forward), jnp.asarray(backward),
        win_col, jnp.asarray(out_map), jnp.asarray(q_table),
    )
    held = (ncol, near, XM, 2 * oc) if early else (8, 128)
    results = pl.pallas_call(
        functools.partial(exchange_kernel, nf, ncol, near, early),
        out_shape=(
            pltpu.VMEM((ncol, nf, 2, XM, width), BF16),
            pltpu.VMEM(held, F32),
            pltpu.VMEM((ncol, 2 * width, 2 * oc), BF16),
            pltpu.SMEM((ncol, 8, lanes), jnp.int32),
        ),
        in_specs=[hbm] * len(operands),
        out_specs=(vmem, vmem, vmem, smem),
        scratch_shapes=[
            pltpu.SMEM((nf,), jnp.int32),
            pltpu.SMEM((nf,), jnp.int32),
            pltpu.VMEM(forward.shape, BF16),
            pltpu.VMEM(backward.shape, BF16),
            pltpu.VMEM(win_col.shape, jnp.int32),
            pltpu.VMEM(strip_blocks.shape, BF16),
            pltpu.VMEM(q_table.shape, BF16),
            pltpu.VMEM(weights.shape, BF16),
            halves,
            halves,
            pltpu.VMEM((xa, width), F32),
            pltpu.VMEM((xa, width), BF16),
            halves,
            pltpu.VMEM((nf, 2 * XM, xa), BF16),
            pltpu.VMEM((8, lanes), jnp.int32),
            pltpu.VMEM((ncol, 8, lanes), jnp.int32),
            pltpu.VMEM(out_map.shape, BF16),
            pltpu.VMEM((2, 2, xa, width), F32),
            dma((CHUNKS + 11,)), dma((2, nf)), dma((2, nf)), dma((2, nf)),
            dma((ncol, nf, 2)), dma((ncol, nf, 2)), dma((ncol, nf, 2)), dma((ncol, nf, 2)),
            dma((ncol,)), dma((ncol,)),
        ],
        compiler_params=pltpu.CompilerParams(
            collective_id=0, has_side_effects=True, vmem_limit_bytes=VMEM_LIMIT
        ),
        name="exchange",
    )(*[pltpu.with_memory_space_constraint(x, pltpu.HBM) for x in operands])
    terms, values, maps, starts_all = results
    spaces = (pltpu.SMEM, pltpu.VMEM, pltpu.VMEM, pltpu.VMEM)
    out = pl.pallas_call(
        functools.partial(finish_kernel, nf, ncol, near, early),
        out_shape=jax.ShapeDtypeStruct((2, own_rows, oc), BF16),
        in_specs=[smem, vmem, vmem, vmem],
        out_specs=hbm,
        scratch_shapes=[
            pltpu.VMEM((own_rows + 2 * XM + ALIGN, 2 * oc), F32),
            pltpu.VMEM((2, own_rows, oc), BF16),
            dma((OUT_CHUNKS,)),
        ],
        compiler_params=pltpu.CompilerParams(vmem_limit_bytes=VMEM_LIMIT),
        name="finish",
    )(*[pltpu.with_memory_space_constraint(x, m) for x, m in zip((starts_all, terms, values, maps), spaces)])
    return out[None]


def solution(mesh):
    in_specs = (
        P("facet", None, None, "col"),
        P(None, "col"),
        P(),
        P(),
        P("facet", None, None, "col"),
    )
    out_specs = P("facet", None, "col", None)
    return jax.shard_map(body, mesh=mesh, in_specs=in_specs, out_specs=out_specs, check_vma=False)
```

```python
import functools
import math

import jax
import jax.numpy as jnp
import numpy as np
from jax import lax
from jax.experimental import pallas as pl
from jax.experimental.pallas import tpu as pltpu
from jax.sharding import PartitionSpec as P

XM = 128
ALIGN = 16
OUT_CHUNKS = 8
VALUES_LIMIT = 16 * 2**20
VMEM_LIMIT = 40 * 2**20
MESH = pl.DeviceIdType.MESH
F32 = jnp.float32
BF16 = jnp.bfloat16


def dft(length, sign, scaling):
    ids = np.arange(length)
    angles = 2.0 * np.pi / length * (ids[:, None] * ids[None, :] % length)
    return np.cos(angles) * scaling, sign * np.sin(angles) * scaling


def stacked(real_part, imag_part, axis):
    return np.concatenate([real_part, imag_part], axis=axis).astype(jnp.bfloat16)


def window_tables(length):
    taper = 0.3 + 0.7 * np.sin(np.pi * (np.arange(length) + 0.5) / length) ** 2
    scaling = 1.0 / math.sqrt(length)
    fwd_re, fwd_im = dft(length, -1.0, scaling)
    back_re, back_im = dft(length, 1.0, scaling)
    forward = stacked(fwd_re * taper[None, :], fwd_im * taper[None, :], 0)
    backward = stacked(back_re * taper[:, None], back_im * taper[:, None], 1)
    return forward, backward


def mm(a, b):
    return jnp.dot(a, b, preferred_element_type=F32)


def iota(shape, dim):
    return lax.broadcasted_iota(jnp.int32, shape, dim)


def one_hot(hit):
    return jnp.where(hit, 1.0, 0.0).astype(BF16)


def exchange_kernel(
    nf, ncol, near, early, starts_in, fac_in, prep, wts, fwd_in, bwd_in, win_in, fmap, qtab,
    terms, values, maps, starts_out,
    starts, fac, fwd, bwd, win, pv, qv, wv, send1, recv1, acc, grid, send2, ctab, svec, sall, fv, wdup,
    ld, s1, r1, s2, sd, sx, sp, ro_near, ro_far, rx_near, rx_far, rp, ss, rs,
):
    me = lax.axis_index("facet")
    c = lax.axis_index("col")
    nx = ncol // 2
    xq, core = lax.div(c, 2), lax.rem(c, 2)
    partner = xq * 2 + 1 - core
    pow2 = nf & (nf - 1) == 0
    blocks = prep.shape[1]
    xa, width = wts.shape[1:]
    half = width // 2
    oc = fmap.shape[0]
    deep = nf <= 8

    bits = [1 << b for b in range((nf - 1).bit_length())] if pow2 else []
    flips = [b - 2 * b * lax.rem(lax.div(me, b), 2) for b in bits]
    across = [lax.rem(xq + q, nx) * 2 + core for q in range(nx)]
    behind = [lax.rem(xq + nx - q, nx) * 2 + core for q in range(nx)]

    def peer(i):
        if not pow2:
            return lax.rem(me + i, nf)
        out = me
        for b, flip in zip(bits, flips):
            if isinstance(i, int):
                out = out + flip if i & b else out
            else:
                out = out + flip * lax.rem(lax.div(i, b), 2)
        return out

    def source(i):
        return peer(i) if pow2 else lax.rem(me + nf - i, nf)

    def each(first, last, step):
        if not deep:
            pl.loop(first, last)(step)
            return
        for i in range(first, last):
            step(i)

    def each_down(first, last, step):
        each(0, last - first, lambda k: step(last - 1 - k))

    barrier = pltpu.get_barrier_semaphore()

    def greet(i):
        pl.semaphore_signal(barrier, inc=1, device_id={"facet": peer(i)}, device_id_type=MESH)

    each(1, nf, greet)

    for i in range(1, ncol):
        pl.semaphore_signal(
            barrier, inc=1, device_id={"col": lax.rem(c + i, ncol)}, device_id_type=MESH
        )

    def greet_across(i):
        for q in range(1, nx):
            pl.semaphore_signal(
                barrier, inc=1, device_id={"facet": peer(i), "col": across[q]}, device_id_type=MESH
            )

    each(1, near, greet_across)

    strip_load = pltpu.make_async_copy(prep, pv, ld.at[0])
    small = [(starts_in, starts), (fac_in, fac), (fwd_in, fwd)]
    later = [(win_in, win), (fmap, fv), (bwd_in, bwd), (wts, wv), (qtab, qv)]
    small = [pltpu.make_async_copy(*pair, ld.at[1 + k]) for k, pair in enumerate(small)]
    later = [pltpu.make_async_copy(*pair, ld.at[4 + k]) for k, pair in enumerate(later)]
    for copy in [*small, strip_load, *later]:
        copy.start()
    win_load, f_load, b_load, w_load, q_load = later
    for copy in small:
        copy.wait()

    lane = iota(svec.shape, 1)
    row = jnp.zeros(svec.shape, jnp.int32)
    svec[...] = lax.fori_loop(0, nf, lambda j, v: jnp.where(lane == j, starts[j], v), row)

    def remote(src, dst, send, recv, **where):
        return pltpu.make_async_remote_copy(
            src_ref=src, dst_ref=dst, send_sem=send, recv_sem=recv,
            device_id=where, device_id_type=MESH,
        )

    def send_first(h, i, far):
        j = peer(i)
        return remote(send1.at[h, j], recv1.at[h, me], s1.at[h], r1.at[h, far], facet=j)

    def own_arrival(h, i, far):
        return ro_far.at[h, i - near] if far else ro_near.at[h]

    def across_arrival(h, i, q, far):
        return rx_far.at[q - 1, h, i - near] if far else rx_near.at[q - 1, h]

    def send_second(h, i, far):
        j = peer(i)
        arrived = own_arrival(h, i, far)
        return remote(send2.at[h, j], terms.at[c, me, h], s2.at[h], arrived, facet=j)

    def send_direct(h, i, q):
        j = peer(i)
        return remote(
            send2.at[h, j], terms.at[c, me, h], sd.at[q - 1, h], across_arrival(h, i, q, 0),
            facet=j, col=across[q],
        )

    def forward_x(h, i, q, far):
        block = terms.at[c, source(i), h]
        arrived = across_arrival(h, i, q, far)
        return remote(block, block, sx.at[q - 1, h], arrived, col=across[q])

    def forward_partner(cc, h, i, far):
        block = terms.at[cc, source(i), h]
        return remote(block, block, sp.at[h], rp.at[far * (1 + h)], col=partner)

    def sent(block, sem):
        remote(block, block, sem, rs.at[0], col=partner).wait_send()

    def received(block, sem):
        remote(block, block, ss.at[0], sem, col=partner).wait_recv()

    row_d = iota((XM, 2 * XM), 1) - iota((XM, 2 * XM), 0)
    fwd_table = fwd[...]

    def contribution(j, dst):
        start = starts[j]
        block = lax.div(start, XM)
        shift = start - block * XM
        above = jnp.where(block + 1 == blocks, 0, block + 1)
        top = jnp.concatenate([pv[0, block], pv[1, block]], axis=1)
        low = jnp.concatenate([pv[0, above], pv[1, above]], axis=1)
        picked = mm(one_hot(row_d == shift), jnp.concatenate([top, low], axis=0))
        prod = mm(fwd_table, picked.astype(BF16))
        re = prod[:XM, :width] - prod[XM:, width:]
        im = prod[:XM, width:] + prod[XM:, :width]
        first = iota(re.shape, 1) < half
        dst[0, j] = jnp.where(first, re, pltpu.roll(im, half, 1)).astype(BF16)
        dst[1, j] = jnp.where(first, pltpu.roll(re, half, 1), im).astype(BF16)

    def window_maps():
        win_load.wait()
        f_load.wait()
        fm = fv[...]
        col_n = iota((oc, width), 0)
        for k in range(ncol):
            m = lax.dot_general(
                one_hot(col_n == win[k : k + 1, :]), fm, (((0,), (0,)), ((), ())),
                preferred_element_type=F32,
            ).astype(BF16)
            m_re, m_im = m[:, :oc], m[:, oc:]
            upper = jnp.concatenate([m_re, m_im], axis=1)
            lower = jnp.concatenate([-m_im, m_re], axis=1)
            maps[k] = jnp.concatenate(
                [upper[:half], lower[:half], upper[half:], lower[half:]], axis=0
            )

    strip_load.wait()
    pl.semaphore_wait(barrier, nf - 1 + ncol - 1 + (near - 1) * (nx - 1))

    def first(i, far):
        contribution(peer(i), send1)
        send_first(0, i, far).start()

    each_down(near, nf, lambda i: first(i, 1))
    each_down(1, near, lambda i: first(i, 0))
    each_down(near, nf, lambda i: send_first(1, i, 1).start())
    each_down(1, near, lambda i: send_first(1, i, 0).start())

    contribution(me, recv1)

    for i in range(1, ncol):
        to = lax.rem(c + i, ncol)
        remote(svec, sall.at[c], ss.at[0], rs.at[0], col=to).start()
    sall[c] = svec[...]
    window_maps()

    b_load.wait()
    turn_d = iota((XM, XM), 0) - iota((XM, XM), 1)
    turn_by = lax.rem(starts[me], ALIGN)
    turn = (turn_d == turn_by) | (turn_d == turn_by - XM)
    turned = mm(one_hot(turn), bwd[...]).astype(BF16)
    turned = jnp.concatenate([turned[:, :XM], turned[:, XM:]], axis=0)
    back_d = iota((XM, xa), 1) - iota((XM, xa), 0)

    @pl.loop(0, nf, unroll=deep)
    def _(j):
        hit = (back_d == fac[j]) | (back_d == fac[j] - xa)
        ctab[j] = mm(turned, one_hot(hit)).astype(BF16)

    w_load.wait()
    near_lane = iota((xa, width), 1) < half
    for p in range(2):
        w = wv[p].astype(F32)
        swapped = pltpu.roll(w, half, 1)
        wdup[0, p] = jnp.where(near_lane, w, swapped)
        wdup[1, p] = jnp.where(near_lane, swapped, w)

    grid_d = iota((xa, XM), 0) - iota((xa, XM), 1)

    def place(h, j):
        hit = (grid_d == fac[j]) | (grid_d == fac[j] - xa)
        return mm(one_hot(hit), recv1[h, j])

    def twist(prod, conj):
        n = prod.shape[0] // 2
        crossed = pltpu.roll(prod[n:], half, 1)
        first = iota(crossed.shape, 1) < half
        minus = jnp.logical_not(first) if conj else first
        return prod[:n] + jnp.where(minus, -crossed, crossed)

    q_load.wait()
    for h in range(2):
        acc[...] = place(h, me)

        def gather(i):
            acc[...] += place(h, source(i))

        received(recv1.at[h, pl.ds(0, near - 1)], r1.at[h, 0])
        each(1, near, gather)
        received(recv1.at[h, pl.ds(0, nf - near)], r1.at[h, 1])
        each(near, nf, gather)

        table = qv[...]
        spectrum = twist(mm(table, acc[...].astype(BF16)), False)
        crossed = wdup[h, 1] * pltpu.roll(spectrum, half, 1)
        weighted = wdup[h, 0] * spectrum + jnp.where(near_lane, -crossed, crossed)
        image = twist(mm(table, weighted.astype(BF16)), True)
        grid[...] = (image * image_gain(nf, xa)).astype(BF16)

        def back(j):
            return twist(mm(ctab[j], grid[...]), False).astype(BF16)

        terms[c, me, h] = back(me)
        for q in range(1, nx):
            forward_x(h, 0, q, 0).start()
        forward_partner(c, h, 0, 0).start()

        def second(i, far):
            j = peer(i)
            send2[h, j] = back(j)
            send_second(h, i, far).start()

        def second_near(i):
            second(i, 0)
            for q in range(1, nx):
                send_direct(h, i, q).start()

        each(1, near, second_near)
        each(near, nf, lambda i: second(i, 1))

    sent(sall.at[pl.ds(0, ncol - 1)], ss.at[0])
    received(sall.at[pl.ds(0, ncol - 1)], rs.at[0])
    starts_copy = pltpu.make_async_copy(sall, starts_out, ld.at[9])
    starts_copy.start()

    def relay_near(h):
        received(terms.at[0, pl.ds(0, near - 1), h], ro_near.at[h])
        each(1, near, lambda i: forward_partner(c, h, i, 0).start())
        for q in range(1, nx):
            received(terms.at[0, pl.ds(0, near), h], rx_near.at[q - 1, h])
            each(0, near, lambda i: forward_partner(behind[q], h, i, 0).start())

    def relay_far(i, h):
        received(terms.at[c, source(i), h], own_arrival(h, i, 1))
        for q in range(1, nx):
            forward_x(h, i, q, 1).start()
        forward_partner(c, h, i, 1).start()

    def relay_across(i, h):
        for q in range(1, nx):
            received(terms.at[behind[q], source(i), h], across_arrival(h, i, q, 1))
            forward_partner(behind[q], h, i, 1).start()

    def relay_both(i):
        relay_far(i, 1)
        relay_across(i, 0)

    def map_near(i):
        j = source(i)
        for k in range(ncol):
            values[k, i] = mm(jnp.concatenate([terms[k, j, 0], terms[k, j, 1]], axis=1), maps[k])

    each(near, nf, lambda i: relay_far(i, 0))
    relay_near(0)
    relay_near(1)
    each(near, nf, relay_both)
    received(terms.at[pl.ds(0, nx), pl.ds(0, near)], rp.at[0])
    if early:
        each(0, near, map_near)
    each(near, nf, lambda i: relay_across(i, 1))
    for h in range(2):
        received(terms.at[pl.ds(0, nx), pl.ds(0, nf - near), h], rp.at[1 + h])

    starts_copy.wait()
    for h in range(2):
        sent(send1.at[h, pl.ds(0, nf - 1)], s1.at[h])
        sent(send2.at[h, pl.ds(0, nf - 1)], s2.at[h])
        sent(terms.at[pl.ds(0, nx), :, h], sp.at[h])
        for q in range(1, nx):
            sent(terms.at[0, pl.ds(0, near - 1), h], sd.at[q - 1, h])
            sent(terms.at[0, pl.ds(0, nf - near + 1), h], sx.at[q - 1, h])


def image_gain(nf, xa):
    return math.sqrt(nf * XM) / math.sqrt(xa)


def finish_kernel(nf, ncol, near, early, starts_all, terms, values, maps, out, acc, stage, osem):
    me = lax.axis_index("facet")
    c = lax.axis_index("col")
    own_rows = out.shape[1]
    oc = out.shape[2]
    total = own_rows * ncol
    base = c * own_rows
    pow2 = nf & (nf - 1) == 0

    def source(i):
        if not pow2:
            return lax.rem(me + nf - i, nf)
        return jnp.bitwise_xor(me, i)

    acc[...] = jnp.zeros_like(acc)
    slot = iota((XM, 2 * oc), 0)
    edge = iota((ALIGN, 2 * oc), 0)

    def gather(first, last, value_of):
        @pl.loop(first * ncol, last * ncol)
        def _(t):
            i, cc = lax.div(t, ncol), lax.rem(t, ncol)
            j = source(i)
            rel = starts_all[cc, 0, j] - base + XM
            rel = jnp.where(rel < 0, rel + total, rel)
            rel = jnp.where(rel >= total, rel - total, rel)

            @pl.when(rel < own_rows + XM)
            def _():
                value = value_of(cc, i, j)
                turn = lax.rem(rel, ALIGN)
                low = pl.multiple_of(rel - turn, ALIGN)
                acc[pl.ds(low, XM), :] += jnp.where(slot >= turn, value, 0.0)
                acc[pl.ds(pl.multiple_of(low + XM, ALIGN), ALIGN), :] += jnp.where(
                    edge < turn, value[:ALIGN], 0.0
                )

    def mapped(cc, i, j):
        return mm(jnp.concatenate([terms[cc, j, 0], terms[cc, j, 1]], axis=1), maps[cc])

    split = near if early else 0
    if early:
        gather(0, split, lambda cc, i, j: values[cc, i])
    gather(split, nf, mapped)

    chunk = own_rows // OUT_CHUNKS
    for k in range(OUT_CHUNKS):
        rows = pl.ds(k * chunk, chunk)
        src = pl.ds(XM + k * chunk, chunk)
        stage[0, rows, :] = acc[src, :oc].astype(BF16)
        stage[1, rows, :] = acc[src, oc:].astype(BF16)
        pltpu.make_async_copy(stage.at[:, rows, :], out.at[:, rows, :], osem.at[0]).start()
    pltpu.make_async_copy(stage, out, osem.at[0]).wait()


def body(prepared, sub_off, fac_off, win_col, vis_weights):
    nf = fac_off.shape[0]
    ncol = lax.axis_size("col")
    facet_strip = prepared[0]
    facet_len, width = facet_strip.shape[1:]
    strip_blocks = facet_strip.reshape(2, facet_len // XM, XM, width)
    weights = vis_weights[0]
    xa = weights.shape[1]
    oc = width * ncol // 2
    own_rows = facet_len // ncol
    starts = sub_off[:, 0]
    lanes = -(-nf // 128) * 128
    near = nf // 2 if nf & (nf - 1) == 0 else 1
    nx = ncol // 2
    early = ncol * near * XM * 2 * oc * 4 <= VALUES_LIMIT

    forward, backward = window_tables(XM)
    q_table = stacked(*dft(xa, -1.0, 1.0 / math.sqrt(nf * XM)), 0)
    out_map = stacked(*dft(oc, 1.0, 1.0 / math.sqrt(2 * oc)), 1)

    smem = pl.BlockSpec(memory_space=pltpu.SMEM)
    vmem = pl.BlockSpec(memory_space=pltpu.VMEM)
    hbm = pl.BlockSpec(memory_space=pl.ANY)
    dma = pltpu.SemaphoreType.DMA
    halves = pltpu.VMEM((2, nf, XM, width), BF16)
    operands = (
        starts, fac_off, strip_blocks, weights, jnp.asarray(forward), jnp.asarray(backward),
        win_col, jnp.asarray(out_map), jnp.asarray(q_table),
    )
    held = (ncol, near, XM, 2 * oc) if early else (8, 128)
    results = pl.pallas_call(
        functools.partial(exchange_kernel, nf, ncol, near, early),
        out_shape=(
            pltpu.VMEM((ncol, nf, 2, XM, width), BF16),
            pltpu.VMEM(held, F32),
            pltpu.VMEM((ncol, 2 * width, 2 * oc), BF16),
            pltpu.SMEM((ncol, 8, lanes), jnp.int32),
        ),
        in_specs=[hbm] * len(operands),
        out_specs=(vmem, vmem, vmem, smem),
        scratch_shapes=[
            pltpu.SMEM((nf,), jnp.int32),
            pltpu.SMEM((nf,), jnp.int32),
            pltpu.VMEM(forward.shape, BF16),
            pltpu.VMEM(backward.shape, BF16),
            pltpu.VMEM(win_col.shape, jnp.int32),
            pltpu.VMEM(strip_blocks.shape, BF16),
            pltpu.VMEM(q_table.shape, BF16),
            pltpu.VMEM(weights.shape, BF16),
            halves,
            halves,
            pltpu.VMEM((xa, width), F32),
            pltpu.VMEM((xa, width), BF16),
            halves,
            pltpu.VMEM((nf, 2 * XM, xa), BF16),
            pltpu.VMEM((8, lanes), jnp.int32),
            pltpu.VMEM((ncol, 8, lanes), jnp.int32),
            pltpu.VMEM(out_map.shape, BF16),
            pltpu.VMEM((2, 2, xa, width), F32),
            dma((10,)), dma((2,)), dma((2, 2)), dma((2,)),
            dma((nx - 1, 2)), dma((nx - 1, 2)), dma((2,)),
            dma((2,)), dma((2, nf - near)), dma((nx - 1, 2)), dma((nx - 1, 2, nf - near)), dma((3,)),
            dma((1,)), dma((1,)),
        ],
        compiler_params=pltpu.CompilerParams(
            collective_id=0, has_side_effects=True, vmem_limit_bytes=VMEM_LIMIT
        ),
        name="exchange",
    )(*[pltpu.with_memory_space_constraint(x, pltpu.HBM) for x in operands])
    terms, values, maps, starts_all = results
    spaces = (pltpu.SMEM, pltpu.VMEM, pltpu.VMEM, pltpu.VMEM)
    out = pl.pallas_call(
        functools.partial(finish_kernel, nf, ncol, near, early),
        out_shape=jax.ShapeDtypeStruct((2, own_rows, oc), BF16),
        in_specs=[smem, vmem, vmem, vmem],
        out_specs=hbm,
        scratch_shapes=[
            pltpu.VMEM((own_rows + 2 * XM + ALIGN, 2 * oc), F32),
            pltpu.VMEM((2, own_rows, oc), BF16),
            dma((1,)),
        ],
        compiler_params=pltpu.CompilerParams(vmem_limit_bytes=VMEM_LIMIT),
        name="finish",
    )(*[pltpu.with_memory_space_constraint(x, m) for x, m in zip((starts_all, terms, values, maps), spaces)])
    return out[None]


def solution(mesh):
    in_specs = (
        P("facet", None, None, "col"),
        P(None, "col"),
        P(),
        P(),
        P("facet", None, None, "col"),
    )
    out_specs = P("facet", None, "col", None)
    return jax.shard_map(body, mesh=mesh, in_specs=in_specs, out_specs=out_specs, check_vma=False)
```

```python
import functools
import math

import jax
import jax.numpy as jnp
import numpy as np
from jax import lax
from jax.experimental import pallas as pl
from jax.experimental.pallas import tpu as pltpu
from jax.sharding import PartitionSpec as P

XM = 128
ALIGN = 16
OUT_CHUNKS = 8
TABLE_LIMIT = 16 * 2**20
VMEM_LIMIT = 40 * 2**20
MESH = pl.DeviceIdType.MESH
F32 = jnp.float32
BF16 = jnp.bfloat16


def dft(length, sign, scaling):
    ids = np.arange(length)
    angles = 2.0 * np.pi / length * (ids[:, None] * ids[None, :] % length)
    return np.cos(angles) * scaling, sign * np.sin(angles) * scaling


def stacked(real_part, imag_part, axis):
    return np.concatenate([real_part, imag_part], axis=axis).astype(jnp.bfloat16)


def window_tables(length):
    taper = 0.3 + 0.7 * np.sin(np.pi * (np.arange(length) + 0.5) / length) ** 2
    scaling = 1.0 / math.sqrt(length)
    fwd_re, fwd_im = dft(length, -1.0, scaling)
    back_re, back_im = dft(length, 1.0, scaling)
    forward = stacked(fwd_re * taper[None, :], fwd_im * taper[None, :], 0)
    backward = stacked(back_re * taper[:, None], back_im * taper[:, None], 1)
    return forward, backward


def mm(a, b):
    return jnp.dot(a, b, preferred_element_type=F32)


def iota(shape, dim):
    return lax.broadcasted_iota(jnp.int32, shape, dim)


def one_hot(hit):
    return jnp.where(hit, 1.0, 0.0).astype(BF16)


def exchange_kernel(
    nf, ncol, near, early, folded, starts_in, fac_in, prep, wts, fwd_in, bwd_in, win_in, fmap, qtab,
    terms, values, maps, starts_out,
    starts, fac, fwd, bwd, win, pv, qv, wv, send1, recv1, acc, send2, places, shifts, ctab, svec, sall, fv, wdup,
    ld, s1, r1, s2, sd, sx, sp, ro_near, ro_far, rx_near, rx_far, rp, ss, rs,
):
    me = lax.axis_index("facet")
    c = lax.axis_index("col")
    nx = ncol // 2
    xq, core = lax.div(c, 2), lax.rem(c, 2)
    partner = xq * 2 + 1 - core
    pow2 = nf & (nf - 1) == 0
    blocks = prep.shape[1]
    xa, width = wts.shape[1:]
    half = width // 2
    oc = fmap.shape[0]
    deep = nf <= 8

    bits = [1 << b for b in range((nf - 1).bit_length())] if pow2 else []
    flips = [b - 2 * b * lax.rem(lax.div(me, b), 2) for b in bits]
    across = [lax.rem(xq + q, nx) * 2 + core for q in range(nx)]
    behind = [lax.rem(xq + nx - q, nx) * 2 + core for q in range(nx)]

    def peer(i):
        if not pow2:
            return lax.rem(me + i, nf)
        out = me
        for b, flip in zip(bits, flips):
            if isinstance(i, int):
                out = out + flip if i & b else out
            else:
                out = out + flip * lax.rem(lax.div(i, b), 2)
        return out

    def source(i):
        return peer(i) if pow2 else lax.rem(me + nf - i, nf)

    def each(first, last, step):
        if not deep:
            pl.loop(first, last)(step)
            return
        for i in range(first, last):
            step(i)

    def each_down(first, last, step):
        each(0, last - first, lambda k: step(last - 1 - k))

    barrier = pltpu.get_barrier_semaphore()

    def greet(i):
        pl.semaphore_signal(barrier, inc=1, device_id={"facet": peer(i)}, device_id_type=MESH)

    each(1, nf, greet)

    for i in range(1, ncol):
        pl.semaphore_signal(
            barrier, inc=1, device_id={"col": lax.rem(c + i, ncol)}, device_id_type=MESH
        )

    def greet_across(i):
        for q in range(1, nx):
            pl.semaphore_signal(
                barrier, inc=1, device_id={"facet": peer(i), "col": across[q]}, device_id_type=MESH
            )

    each(1, near, greet_across)

    strip_load = pltpu.make_async_copy(prep, pv, ld.at[0])
    small = [(starts_in, starts), (fac_in, fac), (fwd_in, fwd)]
    later = [(win_in, win), (fmap, fv), (bwd_in, bwd), (wts, wv), (qtab, qv)]
    small = [pltpu.make_async_copy(*pair, ld.at[1 + k]) for k, pair in enumerate(small)]
    later = [pltpu.make_async_copy(*pair, ld.at[4 + k]) for k, pair in enumerate(later)]
    for copy in [*small, strip_load, *later]:
        copy.start()
    win_load, f_load, b_load, w_load, q_load = later
    for copy in small:
        copy.wait()

    lane = iota(svec.shape, 1)
    row = jnp.zeros(svec.shape, jnp.int32)
    svec[...] = lax.fori_loop(0, nf, lambda j, v: jnp.where(lane == j, starts[j], v), row)

    def remote(src, dst, send, recv, **where):
        return pltpu.make_async_remote_copy(
            src_ref=src, dst_ref=dst, send_sem=send, recv_sem=recv,
            device_id=where, device_id_type=MESH,
        )

    def send_first(h, i, far):
        j = peer(i)
        return remote(send1.at[h, j], recv1.at[h, i], s1.at[h], r1.at[h, far], facet=j)

    def own_arrival(h, i, far):
        return ro_far.at[h, i - near] if far else ro_near.at[h]

    def across_arrival(h, i, q, far):
        return rx_far.at[q - 1, h, i - near] if far else rx_near.at[q - 1, h]

    def send_second(h, i, far):
        j = peer(i)
        arrived = own_arrival(h, i, far)
        return remote(send2.at[h, j], terms.at[c, me, h], s2.at[h], arrived, facet=j)

    def send_direct(h, i, q):
        j = peer(i)
        return remote(
            send2.at[h, j], terms.at[c, me, h], sd.at[q - 1, h], across_arrival(h, i, q, 0),
            facet=j, col=across[q],
        )

    def forward_x(h, i, q, far):
        block = terms.at[c, source(i), h]
        arrived = across_arrival(h, i, q, far)
        return remote(block, block, sx.at[q - 1, h], arrived, col=across[q])

    def forward_partner(cc, h, i, far):
        block = terms.at[cc, source(i), h]
        return remote(block, block, sp.at[h], rp.at[far * (1 + h)], col=partner)

    def sent(block, sem):
        remote(block, block, sem, rs.at[0], col=partner).wait_send()

    def received(block, sem):
        remote(block, block, ss.at[0], sem, col=partner).wait_recv()

    row_d = iota((XM, 2 * XM), 1) - iota((XM, 2 * XM), 0)
    fwd_table = fwd[...]

    def contribution(j, dst, at):
        start = starts[j]
        block = lax.div(start, XM)
        shift = start - block * XM
        above = jnp.where(block + 1 == blocks, 0, block + 1)
        top = jnp.concatenate([pv[0, block], pv[1, block]], axis=1)
        low = jnp.concatenate([pv[0, above], pv[1, above]], axis=1)
        picked = mm(one_hot(row_d == shift), jnp.concatenate([top, low], axis=0))
        prod = mm(fwd_table, picked.astype(BF16))
        re = prod[:XM, :width] - prod[XM:, width:]
        im = prod[:XM, width:] + prod[XM:, :width]
        first = iota(re.shape, 1) < half
        dst[0, at] = jnp.where(first, re, pltpu.roll(im, half, 1)).astype(BF16)
        dst[1, at] = jnp.where(first, pltpu.roll(re, half, 1), im).astype(BF16)

    def window_maps():
        win_load.wait()
        f_load.wait()
        fm = fv[...]
        col_n = iota((oc, width), 0)
        for k in range(ncol):
            m = lax.dot_general(
                one_hot(col_n == win[k : k + 1, :]), fm, (((0,), (0,)), ((), ())),
                preferred_element_type=F32,
            ).astype(BF16)
            m_re, m_im = m[:, :oc], m[:, oc:]
            upper = jnp.concatenate([m_re, m_im], axis=1)
            lower = jnp.concatenate([-m_im, m_re], axis=1)
            maps[k] = jnp.concatenate(
                [upper[:half], lower[:half], upper[half:], lower[half:]], axis=0
            )

    strip_load.wait()
    pl.semaphore_wait(barrier, nf - 1 + ncol - 1 + (near - 1) * (nx - 1))

    def first(i, far):
        contribution(peer(i), send1, peer(i))
        send_first(0, i, far).start()

    each_down(near, nf, lambda i: first(i, 1))
    each_down(1, near, lambda i: first(i, 0))
    each_down(near, nf, lambda i: send_first(1, i, 1).start())
    each_down(1, near, lambda i: send_first(1, i, 0).start())

    contribution(me, recv1, 0)

    for i in range(1, ncol):
        to = lax.rem(c + i, ncol)
        remote(svec, sall.at[c], ss.at[0], rs.at[0], col=to).start()
    sall[c] = svec[...]

    grid_d = iota((xa, XM), 0) - iota((xa, XM), 1)
    back_d = iota((XM, xa), 1) - iota((XM, xa), 0)

    def hit(diff, j):
        return one_hot((diff == fac[j]) | (diff == fac[j] - xa))

    if folded:
        for i in range(nf):
            places[:, i * XM : (i + 1) * XM] = hit(grid_d, source(i))

    w_load.wait()
    near_lane = iota((xa, width), 1) < half
    for p in range(2):
        w = wv[p].astype(F32)
        swapped = pltpu.roll(w, half, 1)
        wdup[0, p] = jnp.where(near_lane, w, swapped)
        wdup[1, p] = jnp.where(near_lane, swapped, w)

    b_load.wait()
    turn_d = iota((XM, XM), 0) - iota((XM, XM), 1)
    turn_by = lax.rem(starts[me], ALIGN)
    turn = (turn_d == turn_by) | (turn_d == turn_by - XM)
    turned = mm(one_hot(turn), bwd[...]).astype(BF16)
    turned = jnp.concatenate([turned[:, :XM], turned[:, XM:]], axis=0)

    q_load.wait()
    column = iota((nf, xa), 0)
    at_row = jnp.zeros((nf, xa), jnp.int32)
    at_row = lax.fori_loop(0, nf, lambda j, v: jnp.where(column == j, fac[j], v), at_row)
    picks = one_hot(iota((nf, xa), 1) == at_row)
    unit = math.sqrt(nf * XM) * image_gain(nf, xa)
    shifts[0] = mm(picks, qv[:xa]) * unit
    shifts[1] = mm(picks, qv[xa:]) * -unit
    with_re = mm(turned, qv[:XM])
    with_im = mm(turned, qv[xa : xa + XM])
    base_re = with_re[:XM] + with_im[XM:]
    base_im = with_re[XM:] - with_im[:XM]

    def back_table(j):
        re, im = shifts[0, pl.ds(j, 1), :], shifts[1, pl.ds(j, 1), :]
        ctab[j, :XM] = (base_re * re - base_im * im).astype(BF16)
        ctab[j, XM:] = (base_re * im + base_im * re).astype(BF16)

    each(0, nf, back_table)

    def twist(prod):
        n = prod.shape[0] // 2
        crossed = pltpu.roll(prod[n:], half, 1)
        first = iota(crossed.shape, 1) < half
        return prod[:n] + jnp.where(first, -crossed, crossed)

    def arrived(h, first, last):
        return recv1[h, first:last].reshape((last - first) * XM, width)

    for h in range(2):
        near_blocks, far_blocks = recv1.at[h, pl.ds(0, near - 1)], recv1.at[h, pl.ds(0, nf - near)]
        if folded:
            split = near * XM
            received(near_blocks, r1.at[h, 0])
            acc[...] = mm(places[:, :split], arrived(h, 0, near))
            received(far_blocks, r1.at[h, 1])
            acc[...] += mm(places[:, split:], arrived(h, near, nf))
        else:
            acc[...] = mm(hit(grid_d, me), recv1[h, 0])

            def gather(i):
                acc[...] += mm(hit(grid_d, source(i)), recv1[h, i])

            received(near_blocks, r1.at[h, 0])
            each(1, near, gather)
            received(far_blocks, r1.at[h, 1])
            each(near, nf, gather)
        prod = mm(qv[...], acc[...].astype(BF16))
        spectrum = twist(prod)
        crossed = wdup[h, 1] * pltpu.roll(spectrum, half, 1)
        weighted = wdup[h, 0] * spectrum + jnp.where(near_lane, -crossed, crossed)
        weighted = weighted.astype(BF16)

        def back(j):
            return twist(mm(ctab[j], weighted)).astype(BF16)

        terms[c, me, h] = back(me)
        for q in range(1, nx):
            forward_x(h, 0, q, 0).start()
        forward_partner(c, h, 0, 0).start()

        def second(i, far):
            j = peer(i)
            send2[h, j] = back(j)
            send_second(h, i, far).start()

        def second_near(i):
            second(i, 0)
            for q in range(1, nx):
                send_direct(h, i, q).start()

        each(1, near, second_near)
        each(near, nf, lambda i: second(i, 1))
        if h == 0:
            window_maps()

    sent(sall.at[pl.ds(0, ncol - 1)], ss.at[0])
    received(sall.at[pl.ds(0, ncol - 1)], rs.at[0])
    starts_copy = pltpu.make_async_copy(sall, starts_out, ld.at[9])
    starts_copy.start()

    def relay_near(h):
        received(terms.at[0, pl.ds(0, near - 1), h], ro_near.at[h])
        each(1, near, lambda i: forward_partner(c, h, i, 0).start())

    def relay_across_near(h):
        for q in range(1, nx):
            received(terms.at[0, pl.ds(0, near), h], rx_near.at[q - 1, h])
            each(0, near, lambda i: forward_partner(behind[q], h, i, 0).start())

    def relay_far(i, h):
        received(terms.at[c, source(i), h], own_arrival(h, i, 1))
        for q in range(1, nx):
            forward_x(h, i, q, 1).start()
        forward_partner(c, h, i, 1).start()

    def relay_across(i, h):
        for q in range(1, nx):
            received(terms.at[behind[q], source(i), h], across_arrival(h, i, q, 1))
            forward_partner(behind[q], h, i, 1).start()

    def relay_both(i):
        relay_far(i, 1)
        relay_across(i, 0)

    def map_near(i):
        j = source(i)
        for k in range(ncol):
            values[k, i] = mm(jnp.concatenate([terms[k, j, 0], terms[k, j, 1]], axis=1), maps[k])

    each(near, nf, lambda i: relay_far(i, 0))
    relay_near(0)
    relay_across_near(0)
    each(near, nf, relay_both)
    relay_near(1)
    relay_across_near(1)
    received(terms.at[pl.ds(0, nx), pl.ds(0, near)], rp.at[0])
    if early:
        each(0, near, map_near)
    each(near, nf, lambda i: relay_across(i, 1))
    for h in range(2):
        received(terms.at[pl.ds(0, nx), pl.ds(0, nf - near), h], rp.at[1 + h])

    starts_copy.wait()
    for h in range(2):
        sent(send1.at[h, pl.ds(0, nf - 1)], s1.at[h])
        sent(send2.at[h, pl.ds(0, nf - 1)], s2.at[h])
        sent(terms.at[pl.ds(0, nx), :, h], sp.at[h])
        for q in range(1, nx):
            sent(terms.at[0, pl.ds(0, near - 1), h], sd.at[q - 1, h])
            sent(terms.at[0, pl.ds(0, nf - near + 1), h], sx.at[q - 1, h])


def image_gain(nf, xa):
    return math.sqrt(nf * XM) / math.sqrt(xa)


def finish_kernel(nf, ncol, near, early, starts_all, terms, values, maps, out, acc, stage, osem):
    me = lax.axis_index("facet")
    c = lax.axis_index("col")
    own_rows = out.shape[1]
    oc = out.shape[2]
    total = own_rows * ncol
    base = c * own_rows
    pow2 = nf & (nf - 1) == 0

    def source(i):
        if not pow2:
            return lax.rem(me + nf - i, nf)
        return jnp.bitwise_xor(me, i)

    acc[...] = jnp.zeros_like(acc)
    slot = iota((XM, 2 * oc), 0)
    edge = iota((ALIGN, 2 * oc), 0)

    def gather(first, last, value_of):
        @pl.loop(first * ncol, last * ncol)
        def _(t):
            i, cc = lax.div(t, ncol), lax.rem(t, ncol)
            j = source(i)
            rel = starts_all[cc, 0, j] - base + XM
            rel = jnp.where(rel < 0, rel + total, rel)
            rel = jnp.where(rel >= total, rel - total, rel)

            @pl.when(rel < own_rows + XM)
            def _():
                value = value_of(cc, i, j)
                turn = lax.rem(rel, ALIGN)
                low = pl.multiple_of(rel - turn, ALIGN)
                acc[pl.ds(low, XM), :] += jnp.where(slot >= turn, value, 0.0)
                acc[pl.ds(pl.multiple_of(low + XM, ALIGN), ALIGN), :] += jnp.where(
                    edge < turn, value[:ALIGN], 0.0
                )

    def mapped(cc, i, j):
        return mm(jnp.concatenate([terms[cc, j, 0], terms[cc, j, 1]], axis=1), maps[cc])

    split = near if early else 0
    if early:
        gather(0, split, lambda cc, i, j: values[cc, i])
    gather(split, nf, mapped)

    chunk = own_rows // OUT_CHUNKS
    for k in range(OUT_CHUNKS):
        rows = pl.ds(k * chunk, chunk)
        src = pl.ds(XM + k * chunk, chunk)
        stage[0, rows, :] = acc[src, :oc].astype(BF16)
        stage[1, rows, :] = acc[src, oc:].astype(BF16)
        pltpu.make_async_copy(stage.at[:, rows, :], out.at[:, rows, :], osem.at[0]).start()
    pltpu.make_async_copy(stage, out, osem.at[0]).wait()


def body(prepared, sub_off, fac_off, win_col, vis_weights):
    nf = fac_off.shape[0]
    ncol = lax.axis_size("col")
    facet_strip = prepared[0]
    facet_len, width = facet_strip.shape[1:]
    strip_blocks = facet_strip.reshape(2, facet_len // XM, XM, width)
    weights = vis_weights[0]
    xa = weights.shape[1]
    oc = width * ncol // 2
    own_rows = facet_len // ncol
    starts = sub_off[:, 0]
    lanes = -(-nf // 128) * 128
    near = nf // 2 if nf & (nf - 1) == 0 else 1
    nx = ncol // 2
    early = ncol * near * XM * 2 * oc * 4 <= TABLE_LIMIT
    folded = xa * nf * XM * 2 <= TABLE_LIMIT // 4

    forward, backward = window_tables(XM)
    q_table = stacked(*dft(xa, -1.0, 1.0 / math.sqrt(nf * XM)), 0)
    out_map = stacked(*dft(oc, 1.0, 1.0 / math.sqrt(2 * oc)), 1)

    smem = pl.BlockSpec(memory_space=pltpu.SMEM)
    vmem = pl.BlockSpec(memory_space=pltpu.VMEM)
    hbm = pl.BlockSpec(memory_space=pl.ANY)
    dma = pltpu.SemaphoreType.DMA
    halves = pltpu.VMEM((2, nf, XM, width), BF16)
    operands = (
        starts, fac_off, strip_blocks, weights, jnp.asarray(forward), jnp.asarray(backward),
        win_col, jnp.asarray(out_map), jnp.asarray(q_table),
    )
    held = (ncol, near, XM, 2 * oc) if early else (8, 128)
    results = pl.pallas_call(
        functools.partial(exchange_kernel, nf, ncol, near, early, folded),
        out_shape=(
            pltpu.VMEM((ncol, nf, 2, XM, width), BF16),
            pltpu.VMEM(held, F32),
            pltpu.VMEM((ncol, 2 * width, 2 * oc), BF16),
            pltpu.SMEM((ncol, 8, lanes), jnp.int32),
        ),
        in_specs=[hbm] * len(operands),
        out_specs=(vmem, vmem, vmem, smem),
        scratch_shapes=[
            pltpu.SMEM((nf,), jnp.int32),
            pltpu.SMEM((nf,), jnp.int32),
            pltpu.VMEM(forward.shape, BF16),
            pltpu.VMEM(backward.shape, BF16),
            pltpu.VMEM(win_col.shape, jnp.int32),
            pltpu.VMEM(strip_blocks.shape, BF16),
            pltpu.VMEM(q_table.shape, BF16),
            pltpu.VMEM(weights.shape, BF16),
            halves,
            halves,
            pltpu.VMEM((xa, width), F32),
            halves,
            pltpu.VMEM((xa, nf * XM) if folded else (8, 128), BF16),
            pltpu.VMEM((2, nf, xa), F32),
            pltpu.VMEM((nf, 2 * XM, xa), BF16),
            pltpu.VMEM((8, lanes), jnp.int32),
            pltpu.VMEM((ncol, 8, lanes), jnp.int32),
            pltpu.VMEM(out_map.shape, BF16),
            pltpu.VMEM((2, 2, xa, width), F32),
            dma((10,)), dma((2,)), dma((2, 2)), dma((2,)),
            dma((nx - 1, 2)), dma((nx - 1, 2)), dma((2,)),
            dma((2,)), dma((2, nf - near)), dma((nx - 1, 2)), dma((nx - 1, 2, nf - near)), dma((3,)),
            dma((1,)), dma((1,)),
        ],
        compiler_params=pltpu.CompilerParams(
            collective_id=0, has_side_effects=True, vmem_limit_bytes=VMEM_LIMIT
        ),
        name="exchange",
    )(*[pltpu.with_memory_space_constraint(x, pltpu.HBM) for x in operands])
    terms, values, maps, starts_all = results
    spaces = (pltpu.SMEM, pltpu.VMEM, pltpu.VMEM, pltpu.VMEM)
    out = pl.pallas_call(
        functools.partial(finish_kernel, nf, ncol, near, early),
        out_shape=jax.ShapeDtypeStruct((2, own_rows, oc), BF16),
        in_specs=[smem, vmem, vmem, vmem],
        out_specs=hbm,
        scratch_shapes=[
            pltpu.VMEM((own_rows + 2 * XM + ALIGN, 2 * oc), F32),
            pltpu.VMEM((2, own_rows, oc), BF16),
            dma((1,)),
        ],
        compiler_params=pltpu.CompilerParams(vmem_limit_bytes=VMEM_LIMIT),
        name="finish",
    )(*[pltpu.with_memory_space_constraint(x, m) for x, m in zip((starts_all, terms, values, maps), spaces)])
    return out[None]


def solution(mesh):
    in_specs = (
        P("facet", None, None, "col"),
        P(None, "col"),
        P(),
        P(),
        P("facet", None, None, "col"),
    )
    out_specs = P("facet", None, "col", None)
    return jax.shard_map(body, mesh=mesh, in_specs=in_specs, out_specs=out_specs, check_vma=False)
```

```python
import functools
import math

import jax
import jax.numpy as jnp
import numpy as np
from jax import lax
from jax.experimental import pallas as pl
from jax.experimental.pallas import tpu as pltpu
from jax.sharding import PartitionSpec as P

XM = 128
ALIGN = 16
OUT_CHUNKS = 8
TABLE_LIMIT = 16 * 2**20
VMEM_LIMIT = 40 * 2**20
MESH = pl.DeviceIdType.MESH
F32 = jnp.float32
BF16 = jnp.bfloat16


def dft(length, sign, scaling):
    ids = np.arange(length)
    angles = 2.0 * np.pi / length * (ids[:, None] * ids[None, :] % length)
    return np.cos(angles) * scaling, sign * np.sin(angles) * scaling


def stacked(real_part, imag_part, axis):
    return np.concatenate([real_part, imag_part], axis=axis).astype(jnp.bfloat16)


def window_tables(length):
    taper = 0.3 + 0.7 * np.sin(np.pi * (np.arange(length) + 0.5) / length) ** 2
    scaling = 1.0 / math.sqrt(length)
    fwd_re, fwd_im = dft(length, -1.0, scaling)
    back_re, back_im = dft(length, 1.0, scaling)
    forward = stacked(fwd_re * taper[None, :], fwd_im * taper[None, :], 0)
    backward = stacked(back_re * taper[:, None], back_im * taper[:, None], 1)
    return forward, backward


def mm(a, b):
    return jnp.dot(a, b, preferred_element_type=F32)


def iota(shape, dim):
    return lax.broadcasted_iota(jnp.int32, shape, dim)


def one_hot(hit):
    return jnp.where(hit, 1.0, 0.0).astype(BF16)


def exchange_kernel(
    nf, ncol, near, early, folded, starts_in, fac_in, prep, wts, fwd_in, bwd_in, win_in, fmap, qtab,
    terms, values, maps, starts_out,
    starts, fac, fwd, bwd, win, pv, qv, wv, send1, recv1, acc, send2, places, shifts, ctab, svec, sall, fv, wdup,
    ld, s1, r1, s2, sd, sx, sp, ro_near, ro_far, rx_near, rx_far, rp, ss, rs,
):
    me = lax.axis_index("facet")
    c = lax.axis_index("col")
    nx = ncol // 2
    xq, core = lax.div(c, 2), lax.rem(c, 2)
    partner = xq * 2 + 1 - core
    pow2 = nf & (nf - 1) == 0
    blocks = prep.shape[1]
    xa, width = wts.shape[1:]
    half = width // 2
    oc = fmap.shape[0]
    deep = nf <= 8

    bits = [1 << b for b in range((nf - 1).bit_length())] if pow2 else []
    flips = [b - 2 * b * lax.rem(lax.div(me, b), 2) for b in bits]
    across = [lax.rem(xq + q, nx) * 2 + core for q in range(nx)]
    behind = [lax.rem(xq + nx - q, nx) * 2 + core for q in range(nx)]

    def peer(i):
        if not pow2:
            return lax.rem(me + i, nf)
        out = me
        for b, flip in zip(bits, flips):
            if isinstance(i, int):
                out = out + flip if i & b else out
            else:
                out = out + flip * lax.rem(lax.div(i, b), 2)
        return out

    def source(i):
        return peer(i) if pow2 else lax.rem(me + nf - i, nf)

    def each(first, last, step):
        if not deep:
            pl.loop(first, last)(step)
            return
        for i in range(first, last):
            step(i)

    def each_down(first, last, step):
        each(0, last - first, lambda k: step(last - 1 - k))

    barrier = pltpu.get_barrier_semaphore()

    def greet(i):
        pl.semaphore_signal(barrier, inc=1, device_id={"facet": peer(i)}, device_id_type=MESH)

    each(1, nf, greet)

    for i in range(1, ncol):
        pl.semaphore_signal(
            barrier, inc=1, device_id={"col": lax.rem(c + i, ncol)}, device_id_type=MESH
        )

    def greet_across(i):
        for q in range(1, nx):
            pl.semaphore_signal(
                barrier, inc=1, device_id={"facet": peer(i), "col": across[q]}, device_id_type=MESH
            )

    each(1, near, greet_across)

    strip_load = pltpu.make_async_copy(prep, pv, ld.at[0])
    small = [(starts_in, starts), (fac_in, fac), (fwd_in, fwd)]
    later = [(win_in, win), (fmap, fv), (bwd_in, bwd), (wts, wv), (qtab, qv)]
    small = [pltpu.make_async_copy(*pair, ld.at[1 + k]) for k, pair in enumerate(small)]
    later = [pltpu.make_async_copy(*pair, ld.at[4 + k]) for k, pair in enumerate(later)]
    for copy in [*small, strip_load, *later]:
        copy.start()
    win_load, f_load, b_load, w_load, q_load = later
    for copy in small:
        copy.wait()

    lane = iota(svec.shape, 1)
    row = jnp.zeros(svec.shape, jnp.int32)
    svec[...] = lax.fori_loop(0, nf, lambda j, v: jnp.where(lane == j, starts[j], v), row)

    def remote(src, dst, send, recv, **where):
        return pltpu.make_async_remote_copy(
            src_ref=src, dst_ref=dst, send_sem=send, recv_sem=recv,
            device_id=where, device_id_type=MESH,
        )

    def send_first(h, i, far):
        j = peer(i)
        return remote(send1.at[h, j], recv1.at[h, i], s1.at[h], r1.at[h, far], facet=j)

    def own_arrival(h, i, far):
        return ro_far.at[h, i - near] if far else ro_near.at[h]

    def across_arrival(h, i, q, far):
        return rx_far.at[q - 1, h, i - near] if far else rx_near.at[q - 1, h]

    def send_second(h, i, far):
        j = peer(i)
        arrived = own_arrival(h, i, far)
        return remote(send2.at[h, j], terms.at[c, me, h], s2.at[h], arrived, facet=j)

    def send_direct(h, i, q):
        j = peer(i)
        return remote(
            send2.at[h, j], terms.at[c, me, h], sd.at[q - 1, h], across_arrival(h, i, q, 0),
            facet=j, col=across[q],
        )

    def forward_x(h, i, q, far):
        block = terms.at[c, source(i), h]
        arrived = across_arrival(h, i, q, far)
        return remote(block, block, sx.at[q - 1, h], arrived, col=across[q])

    def forward_partner(cc, h, i, far):
        block = terms.at[cc, source(i), h]
        return remote(block, block, sp.at[h], rp.at[far * (1 + h)], col=partner)

    def sent(block, sem):
        remote(block, block, sem, rs.at[0], col=partner).wait_send()

    def received(block, sem):
        remote(block, block, ss.at[0], sem, col=partner).wait_recv()

    row_d = iota((XM, 2 * XM), 1) - iota((XM, 2 * XM), 0)
    fwd_table = fwd[...]

    def contribution(j, dst, at):
        start = starts[j]
        block = lax.div(start, XM)
        shift = start - block * XM
        above = jnp.where(block + 1 == blocks, 0, block + 1)
        top = jnp.concatenate([pv[0, block], pv[1, block]], axis=1)
        low = jnp.concatenate([pv[0, above], pv[1, above]], axis=1)
        picked = mm(one_hot(row_d == shift), jnp.concatenate([top, low], axis=0))
        prod = mm(fwd_table, picked.astype(BF16))
        re = prod[:XM, :width] - prod[XM:, width:]
        im = prod[:XM, width:] + prod[XM:, :width]
        first = iota(re.shape, 1) < half
        dst[0, at] = jnp.where(first, re, pltpu.roll(im, half, 1)).astype(BF16)
        dst[1, at] = jnp.where(first, pltpu.roll(re, half, 1), im).astype(BF16)

    def window_maps():
        win_load.wait()
        f_load.wait()
        fm = fv[...]
        col_n = iota((oc, width), 0)
        for k in range(ncol):
            m = lax.dot_general(
                one_hot(col_n == win[k : k + 1, :]), fm, (((0,), (0,)), ((), ())),
                preferred_element_type=F32,
            ).astype(BF16)
            m_re, m_im = m[:, :oc], m[:, oc:]
            upper = jnp.concatenate([m_re, m_im], axis=1)
            lower = jnp.concatenate([-m_im, m_re], axis=1)
            maps[k] = jnp.concatenate(
                [upper[:half], lower[:half], upper[half:], lower[half:]], axis=0
            )

    strip_load.wait()
    pl.semaphore_wait(barrier, nf - 1 + ncol - 1 + (near - 1) * (nx - 1))

    def first(i, far):
        contribution(peer(i), send1, peer(i))
        send_first(0, i, far).start()

    each_down(near, nf, lambda i: first(i, 1))
    each_down(1, near, lambda i: first(i, 0))

    contribution(me, recv1, 0)

    for i in range(1, ncol):
        to = lax.rem(c + i, ncol)
        remote(svec, sall.at[c], ss.at[0], rs.at[0], col=to).start()
    sall[c] = svec[...]

    grid_d = iota((xa, XM), 0) - iota((xa, XM), 1)
    back_d = iota((XM, xa), 1) - iota((XM, xa), 0)

    def hit(diff, j):
        return one_hot((diff == fac[j]) | (diff == fac[j] - xa))

    if folded:
        for i in range(nf):
            places[:, i * XM : (i + 1) * XM] = hit(grid_d, source(i))

    w_load.wait()
    near_lane = iota((xa, width), 1) < half
    for p in range(2):
        w = wv[p].astype(F32)
        swapped = pltpu.roll(w, half, 1)
        wdup[0, p] = jnp.where(near_lane, w, swapped)
        wdup[1, p] = jnp.where(near_lane, swapped, w)

    b_load.wait()
    turn_d = iota((XM, XM), 0) - iota((XM, XM), 1)
    turn_by = lax.rem(starts[me], ALIGN)
    turn = (turn_d == turn_by) | (turn_d == turn_by - XM)
    turned = mm(one_hot(turn), bwd[...]).astype(BF16)
    turned = jnp.concatenate([turned[:, :XM], turned[:, XM:]], axis=0)

    q_load.wait()
    column = iota((nf, xa), 0)
    at_row = jnp.zeros((nf, xa), jnp.int32)
    at_row = lax.fori_loop(0, nf, lambda j, v: jnp.where(column == j, fac[j], v), at_row)
    picks = one_hot(iota((nf, xa), 1) == at_row)
    unit = math.sqrt(nf * XM) * image_gain(nf, xa)
    shifts[0] = mm(picks, qv[:xa]) * unit
    shifts[1] = mm(picks, qv[xa:]) * -unit
    with_re = mm(turned, qv[:XM])
    with_im = mm(turned, qv[xa : xa + XM])
    base_re = with_re[:XM] + with_im[XM:]
    base_im = with_re[XM:] - with_im[:XM]

    def back_table(j):
        re, im = shifts[0, pl.ds(j, 1), :], shifts[1, pl.ds(j, 1), :]
        ctab[j, :XM] = (base_re * re - base_im * im).astype(BF16)
        ctab[j, XM:] = (base_re * im + base_im * re).astype(BF16)

    each(0, nf, back_table)

    sent(send1.at[0, pl.ds(0, nf - 1)], s1.at[0])
    each_down(near, nf, lambda i: send_first(1, i, 1).start())
    each_down(1, near, lambda i: send_first(1, i, 0).start())

    def twist(prod):
        n = prod.shape[0] // 2
        crossed = pltpu.roll(prod[n:], half, 1)
        first = iota(crossed.shape, 1) < half
        return prod[:n] + jnp.where(first, -crossed, crossed)

    def arrived(h, first, last):
        return recv1[h, first:last].reshape((last - first) * XM, width)

    for h in range(2):
        near_blocks, far_blocks = recv1.at[h, pl.ds(0, near - 1)], recv1.at[h, pl.ds(0, nf - near)]
        if folded:
            split = near * XM
            received(near_blocks, r1.at[h, 0])
            acc[...] = mm(places[:, :split], arrived(h, 0, near))
            received(far_blocks, r1.at[h, 1])
            acc[...] += mm(places[:, split:], arrived(h, near, nf))
        else:
            acc[...] = mm(hit(grid_d, me), recv1[h, 0])

            def gather(i):
                acc[...] += mm(hit(grid_d, source(i)), recv1[h, i])

            received(near_blocks, r1.at[h, 0])
            each(1, near, gather)
            received(far_blocks, r1.at[h, 1])
            each(near, nf, gather)
        prod = mm(qv[...], acc[...].astype(BF16))
        spectrum = twist(prod)
        crossed = wdup[h, 1] * pltpu.roll(spectrum, half, 1)
        weighted = wdup[h, 0] * spectrum + jnp.where(near_lane, -crossed, crossed)
        weighted = weighted.astype(BF16)

        def back(j):
            return twist(mm(ctab[j], weighted)).astype(BF16)

        terms[c, me, h] = back(me)
        for q in range(1, nx):
            forward_x(h, 0, q, 0).start()
        forward_partner(c, h, 0, 0).start()

        def second(i, far):
            j = peer(i)
            send2[h, j] = back(j)
            send_second(h, i, far).start()

        def second_near(i):
            second(i, 0)
            for q in range(1, nx):
                send_direct(h, i, q).start()

        each(1, near, second_near)
        each(near, nf, lambda i: second(i, 1))
        if h == 0:
            window_maps()

    sent(sall.at[pl.ds(0, ncol - 1)], ss.at[0])
    received(sall.at[pl.ds(0, ncol - 1)], rs.at[0])
    starts_copy = pltpu.make_async_copy(sall, starts_out, ld.at[9])
    starts_copy.start()

    def relay_near(h):
        received(terms.at[0, pl.ds(0, near - 1), h], ro_near.at[h])
        each(1, near, lambda i: forward_partner(c, h, i, 0).start())

    def relay_across_near(h):
        for q in range(1, nx):
            received(terms.at[0, pl.ds(0, near), h], rx_near.at[q - 1, h])
            each(0, near, lambda i: forward_partner(behind[q], h, i, 0).start())

    def relay_far(i, h):
        received(terms.at[c, source(i), h], own_arrival(h, i, 1))
        for q in range(1, nx):
            forward_x(h, i, q, 1).start()
        forward_partner(c, h, i, 1).start()

    def relay_across(i, h):
        for q in range(1, nx):
            received(terms.at[behind[q], source(i), h], across_arrival(h, i, q, 1))
            forward_partner(behind[q], h, i, 1).start()

    def relay_both(i):
        relay_far(i, 1)
        relay_across(i, 0)

    def map_near(i):
        j = source(i)
        for k in range(ncol):
            values[k, i] = mm(jnp.concatenate([terms[k, j, 0], terms[k, j, 1]], axis=1), maps[k])

    each(near, nf, lambda i: relay_far(i, 0))
    relay_near(0)
    relay_near(1)
    relay_across_near(0)
    relay_across_near(1)
    received(terms.at[pl.ds(0, nx), pl.ds(0, near)], rp.at[0])
    def relay_map(i):
        relay_both(i)
        if early:
            map_near(i - near)

    each(near, nf, relay_map)
    each(near, nf, lambda i: relay_across(i, 1))
    for h in range(2):
        received(terms.at[pl.ds(0, nx), pl.ds(0, nf - near), h], rp.at[1 + h])

    starts_copy.wait()
    for h in range(2):
        if h:
            sent(send1.at[h, pl.ds(0, nf - 1)], s1.at[h])
        sent(send2.at[h, pl.ds(0, nf - 1)], s2.at[h])
        sent(terms.at[pl.ds(0, nx), :, h], sp.at[h])
        for q in range(1, nx):
            sent(terms.at[0, pl.ds(0, near - 1), h], sd.at[q - 1, h])
            sent(terms.at[0, pl.ds(0, nf - near + 1), h], sx.at[q - 1, h])


def image_gain(nf, xa):
    return math.sqrt(nf * XM) / math.sqrt(xa)


def finish_kernel(nf, ncol, near, early, starts_all, terms, values, maps, out, acc, stage, osem):
    me = lax.axis_index("facet")
    c = lax.axis_index("col")
    own_rows = out.shape[1]
    oc = out.shape[2]
    total = own_rows * ncol
    base = c * own_rows
    pow2 = nf & (nf - 1) == 0

    def source(i):
        if not pow2:
            return lax.rem(me + nf - i, nf)
        return jnp.bitwise_xor(me, i)

    acc[...] = jnp.zeros_like(acc)
    slot = iota((XM, 2 * oc), 0)
    edge = iota((ALIGN, 2 * oc), 0)

    def gather(first, last, value_of):
        @pl.loop(first * ncol, last * ncol)
        def _(t):
            i, cc = lax.div(t, ncol), lax.rem(t, ncol)
            j = source(i)
            rel = starts_all[cc, 0, j] - base + XM
            rel = jnp.where(rel < 0, rel + total, rel)
            rel = jnp.where(rel >= total, rel - total, rel)

            @pl.when(rel < own_rows + XM)
            def _():
                value = value_of(cc, i, j)
                turn = lax.rem(rel, ALIGN)
                low = pl.multiple_of(rel - turn, ALIGN)
                acc[pl.ds(low, XM), :] += jnp.where(slot >= turn, value, 0.0)
                acc[pl.ds(pl.multiple_of(low + XM, ALIGN), ALIGN), :] += jnp.where(
                    edge < turn, value[:ALIGN], 0.0
                )

    def mapped(cc, i, j):
        return mm(jnp.concatenate([terms[cc, j, 0], terms[cc, j, 1]], axis=1), maps[cc])

    split = near if early else 0
    if early:
        gather(0, split, lambda cc, i, j: values[cc, i])
    gather(split, nf, mapped)

    chunk = own_rows // OUT_CHUNKS
    for k in range(OUT_CHUNKS):
        rows = pl.ds(k * chunk, chunk)
        src = pl.ds(XM + k * chunk, chunk)
        stage[0, rows, :] = acc[src, :oc].astype(BF16)
        stage[1, rows, :] = acc[src, oc:].astype(BF16)
        pltpu.make_async_copy(stage.at[:, rows, :], out.at[:, rows, :], osem.at[0]).start()
    pltpu.make_async_copy(stage, out, osem.at[0]).wait()


def body(prepared, sub_off, fac_off, win_col, vis_weights):
    nf = fac_off.shape[0]
    ncol = lax.axis_size("col")
    facet_strip = prepared[0]
    facet_len, width = facet_strip.shape[1:]
    strip_blocks = facet_strip.reshape(2, facet_len // XM, XM, width)
    weights = vis_weights[0]
    xa = weights.shape[1]
    oc = width * ncol // 2
    own_rows = facet_len // ncol
    starts = sub_off[:, 0]
    lanes = -(-nf // 128) * 128
    near = nf // 2 if nf & (nf - 1) == 0 else 1
    nx = ncol // 2
    early = ncol * near * XM * 2 * oc * 4 <= TABLE_LIMIT
    folded = xa * nf * XM * 2 <= TABLE_LIMIT // 4

    forward, backward = window_tables(XM)
    q_table = stacked(*dft(xa, -1.0, 1.0 / math.sqrt(nf * XM)), 0)
    out_map = stacked(*dft(oc, 1.0, 1.0 / math.sqrt(2 * oc)), 1)

    smem = pl.BlockSpec(memory_space=pltpu.SMEM)
    vmem = pl.BlockSpec(memory_space=pltpu.VMEM)
    hbm = pl.BlockSpec(memory_space=pl.ANY)
    dma = pltpu.SemaphoreType.DMA
    halves = pltpu.VMEM((2, nf, XM, width), BF16)
    operands = (
        starts, fac_off, strip_blocks, weights, jnp.asarray(forward), jnp.asarray(backward),
        win_col, jnp.asarray(out_map), jnp.asarray(q_table),
    )
    held = (ncol, near, XM, 2 * oc) if early else (8, 128)
    results = pl.pallas_call(
        functools.partial(exchange_kernel, nf, ncol, near, early, folded),
        out_shape=(
            pltpu.VMEM((ncol, nf, 2, XM, width), BF16),
            pltpu.VMEM(held, F32),
            pltpu.VMEM((ncol, 2 * width, 2 * oc), BF16),
            pltpu.SMEM((ncol, 8, lanes), jnp.int32),
        ),
        in_specs=[hbm] * len(operands),
        out_specs=(vmem, vmem, vmem, smem),
        scratch_shapes=[
            pltpu.SMEM((nf,), jnp.int32),
            pltpu.SMEM((nf,), jnp.int32),
            pltpu.VMEM(forward.shape, BF16),
            pltpu.VMEM(backward.shape, BF16),
            pltpu.VMEM(win_col.shape, jnp.int32),
            pltpu.VMEM(strip_blocks.shape, BF16),
            pltpu.VMEM(q_table.shape, BF16),
            pltpu.VMEM(weights.shape, BF16),
            halves,
            halves,
            pltpu.VMEM((xa, width), F32),
            halves,
            pltpu.VMEM((xa, nf * XM) if folded else (8, 128), BF16),
            pltpu.VMEM((2, nf, xa), F32),
            pltpu.VMEM((nf, 2 * XM, xa), BF16),
            pltpu.VMEM((8, lanes), jnp.int32),
            pltpu.VMEM((ncol, 8, lanes), jnp.int32),
            pltpu.VMEM(out_map.shape, BF16),
            pltpu.VMEM((2, 2, xa, width), F32),
            dma((10,)), dma((2,)), dma((2, 2)), dma((2,)),
            dma((nx - 1, 2)), dma((nx - 1, 2)), dma((2,)),
            dma((2,)), dma((2, nf - near)), dma((nx - 1, 2)), dma((nx - 1, 2, nf - near)), dma((3,)),
            dma((1,)), dma((1,)),
        ],
        compiler_params=pltpu.CompilerParams(
            collective_id=0, has_side_effects=True, vmem_limit_bytes=VMEM_LIMIT
        ),
        name="exchange",
    )(*[pltpu.with_memory_space_constraint(x, pltpu.HBM) for x in operands])
    terms, values, maps, starts_all = results
    spaces = (pltpu.SMEM, pltpu.VMEM, pltpu.VMEM, pltpu.VMEM)
    out = pl.pallas_call(
        functools.partial(finish_kernel, nf, ncol, near, early),
        out_shape=jax.ShapeDtypeStruct((2, own_rows, oc), BF16),
        in_specs=[smem, vmem, vmem, vmem],
        out_specs=hbm,
        scratch_shapes=[
            pltpu.VMEM((own_rows + 2 * XM + ALIGN, 2 * oc), F32),
            pltpu.VMEM((2, own_rows, oc), BF16),
            dma((1,)),
        ],
        compiler_params=pltpu.CompilerParams(vmem_limit_bytes=VMEM_LIMIT),
        name="finish",
    )(*[pltpu.with_memory_space_constraint(x, m) for x, m in zip((starts_all, terms, values, maps), spaces)])
    return out[None]


def solution(mesh):
    in_specs = (
        P("facet", None, None, "col"),
        P(None, "col"),
        P(),
        P(),
        P("facet", None, None, "col"),
    )
    out_specs = P("facet", None, "col", None)
    return jax.shard_map(body, mesh=mesh, in_specs=in_specs, out_specs=out_specs, check_vma=False)
```

```python
import functools
import math

import jax
import jax.numpy as jnp
import numpy as np
from jax import lax
from jax.experimental import pallas as pl
from jax.experimental.pallas import tpu as pltpu
from jax.sharding import PartitionSpec as P

XM = 128
ALIGN = 16
OUT_CHUNKS = 8
TABLE_LIMIT = 16 * 2**20
VMEM_LIMIT = 40 * 2**20
MESH = pl.DeviceIdType.MESH
F32 = jnp.float32
BF16 = jnp.bfloat16


def dft(length, sign, scaling):
    ids = np.arange(length)
    angles = 2.0 * np.pi / length * (ids[:, None] * ids[None, :] % length)
    return np.cos(angles) * scaling, sign * np.sin(angles) * scaling


def stacked(real_part, imag_part, axis):
    return np.concatenate([real_part, imag_part], axis=axis).astype(jnp.bfloat16)


def window_tables(length):
    taper = 0.3 + 0.7 * np.sin(np.pi * (np.arange(length) + 0.5) / length) ** 2
    scaling = 1.0 / math.sqrt(length)
    fwd_re, fwd_im = dft(length, -1.0, scaling)
    back_re, back_im = dft(length, 1.0, scaling)
    forward = stacked(fwd_re * taper[None, :], fwd_im * taper[None, :], 0)
    backward = stacked(back_re * taper[:, None], back_im * taper[:, None], 1)
    return forward, backward


def mm(a, b):
    return jnp.dot(a, b, preferred_element_type=F32)


def iota(shape, dim):
    return lax.broadcasted_iota(jnp.int32, shape, dim)


def one_hot(hit):
    return jnp.where(hit, 1.0, 0.0).astype(BF16)


def exchange_kernel(
    nf, ncol, near, early, folded, starts_in, fac_in, prep, wts, fwd_in, bwd_in, win_in, fmap, qtab,
    terms, values, maps, starts_out,
    starts, fac, fwd, bwd, win, pv, qv, wv, send1, recv1, acc, send2, places, shifts, ctab, svec, sall, fv, wdup,
    ld, s1, r1, s2, sd, sx, sp, ro_near, ro_far, rx_near, rx_far, rp, ss, rs,
):
    me = lax.axis_index("facet")
    c = lax.axis_index("col")
    nx = ncol // 2
    xq, core = lax.div(c, 2), lax.rem(c, 2)
    partner = xq * 2 + 1 - core
    pow2 = nf & (nf - 1) == 0
    blocks = prep.shape[1]
    xa, width = wts.shape[1:]
    half = width // 2
    oc = fmap.shape[0]
    deep = nf <= 8

    bits = [1 << b for b in range((nf - 1).bit_length())] if pow2 else []
    flips = [b - 2 * b * lax.rem(lax.div(me, b), 2) for b in bits]
    across = [lax.rem(xq + q, nx) * 2 + core for q in range(nx)]
    behind = [lax.rem(xq + nx - q, nx) * 2 + core for q in range(nx)]

    def peer(i):
        if not pow2:
            return lax.rem(me + i, nf)
        out = me
        for b, flip in zip(bits, flips):
            if isinstance(i, int):
                out = out + flip if i & b else out
            else:
                out = out + flip * lax.rem(lax.div(i, b), 2)
        return out

    def source(i):
        return peer(i) if pow2 else lax.rem(me + nf - i, nf)

    def each(first, last, step):
        if not deep:
            pl.loop(first, last)(step)
            return
        for i in range(first, last):
            step(i)

    def each_down(first, last, step):
        each(0, last - first, lambda k: step(last - 1 - k))

    barrier = pltpu.get_barrier_semaphore()

    def greet(i):
        pl.semaphore_signal(barrier, inc=1, device_id={"facet": peer(i)}, device_id_type=MESH)

    each(1, nf, greet)

    for i in range(1, ncol):
        pl.semaphore_signal(
            barrier, inc=1, device_id={"col": lax.rem(c + i, ncol)}, device_id_type=MESH
        )

    def greet_across(i):
        for q in range(1, nx):
            pl.semaphore_signal(
                barrier, inc=1, device_id={"facet": peer(i), "col": across[q]}, device_id_type=MESH
            )

    each(1, near, greet_across)

    strip_load = pltpu.make_async_copy(prep, pv, ld.at[0])
    small = [(starts_in, starts), (fac_in, fac), (fwd_in, fwd)]
    later = [(win_in, win), (fmap, fv), (bwd_in, bwd), (wts, wv), (qtab, qv)]
    small = [pltpu.make_async_copy(*pair, ld.at[1 + k]) for k, pair in enumerate(small)]
    later = [pltpu.make_async_copy(*pair, ld.at[4 + k]) for k, pair in enumerate(later)]
    for copy in [*small, strip_load, *later]:
        copy.start()
    win_load, f_load, b_load, w_load, q_load = later
    for copy in small:
        copy.wait()

    lane = iota(svec.shape, 1)
    row = jnp.zeros(svec.shape, jnp.int32)
    svec[...] = lax.fori_loop(0, nf, lambda j, v: jnp.where(lane == j, starts[j], v), row)

    def remote(src, dst, send, recv, **where):
        return pltpu.make_async_remote_copy(
            src_ref=src, dst_ref=dst, send_sem=send, recv_sem=recv,
            device_id=where, device_id_type=MESH,
        )

    def send_first(h, i, far):
        j = peer(i)
        return remote(send1.at[h, j], recv1.at[h, i], s1.at[h], r1.at[h, far], facet=j)

    def own_arrival(h, i, far):
        return ro_far.at[h, i - near] if far else ro_near.at[h]

    def across_arrival(h, i, q, far):
        return rx_far.at[q - 1, h, i - near] if far else rx_near.at[q - 1, h]

    def send_second(h, i, far):
        j = peer(i)
        arrived = own_arrival(h, i, far)
        return remote(send2.at[h, j], terms.at[c, me, h], s2.at[h], arrived, facet=j)

    def send_direct(h, i, q):
        j = peer(i)
        return remote(
            send2.at[h, j], terms.at[c, me, h], sd.at[q - 1, h], across_arrival(h, i, q, 0),
            facet=j, col=across[q],
        )

    def forward_x(h, i, q, far):
        block = terms.at[c, source(i), h]
        arrived = across_arrival(h, i, q, far)
        return remote(block, block, sx.at[q - 1, h], arrived, col=across[q])

    def forward_partner(cc, h, i, far):
        block = terms.at[cc, source(i), h]
        return remote(block, block, sp.at[h], rp.at[far * (1 + h)], col=partner)

    def sent(block, sem):
        remote(block, block, sem, rs.at[0], col=partner).wait_send()

    def received(block, sem):
        remote(block, block, ss.at[0], sem, col=partner).wait_recv()

    row_d = iota((XM, 2 * XM), 1) - iota((XM, 2 * XM), 0)
    fwd_table = fwd[...]

    def contribution(j, dst, at):
        start = starts[j]
        block = lax.div(start, XM)
        shift = start - block * XM
        above = jnp.where(block + 1 == blocks, 0, block + 1)
        top = jnp.concatenate([pv[0, block], pv[1, block]], axis=1)
        low = jnp.concatenate([pv[0, above], pv[1, above]], axis=1)
        picked = mm(one_hot(row_d == shift), jnp.concatenate([top, low], axis=0))
        prod = mm(fwd_table, picked.astype(BF16))
        re = prod[:XM, :width] - prod[XM:, width:]
        im = prod[:XM, width:] + prod[XM:, :width]
        first = iota(re.shape, 1) < half
        dst[0, at] = jnp.where(first, re, pltpu.roll(im, half, 1)).astype(BF16)
        dst[1, at] = jnp.where(first, pltpu.roll(re, half, 1), im).astype(BF16)

    def window_maps():
        win_load.wait()
        f_load.wait()
        fm = fv[...]
        col_n = iota((oc, width), 0)
        for k in range(ncol):
            m = lax.dot_general(
                one_hot(col_n == win[k : k + 1, :]), fm, (((0,), (0,)), ((), ())),
                preferred_element_type=F32,
            ).astype(BF16)
            m_re, m_im = m[:, :oc], m[:, oc:]
            upper = jnp.concatenate([m_re, m_im], axis=1)
            lower = jnp.concatenate([-m_im, m_re], axis=1)
            maps[k] = jnp.concatenate(
                [upper[:half], lower[:half], upper[half:], lower[half:]], axis=0
            )

    strip_load.wait()
    pl.semaphore_wait(barrier, nf - 1 + ncol - 1 + (near - 1) * (nx - 1))

    def first(i, far):
        contribution(peer(i), send1, peer(i))
        send_first(0, i, far).start()

    each_down(near, nf, lambda i: first(i, 1))
    each_down(1, near, lambda i: first(i, 0))

    contribution(me, recv1, 0)

    for i in range(1, ncol):
        to = lax.rem(c + i, ncol)
        remote(svec, sall.at[c], ss.at[0], rs.at[0], col=to).start()
    sall[c] = svec[...]

    grid_d = iota((xa, XM), 0) - iota((xa, XM), 1)
    back_d = iota((XM, xa), 1) - iota((XM, xa), 0)

    def hit(diff, j):
        return one_hot((diff == fac[j]) | (diff == fac[j] - xa))

    if folded:
        for i in range(nf):
            places[:, i * XM : (i + 1) * XM] = hit(grid_d, source(i))

    w_load.wait()
    near_lane = iota((xa, width), 1) < half
    for p in range(2):
        w = wv[p].astype(F32)
        swapped = pltpu.roll(w, half, 1)
        wdup[0, p] = jnp.where(near_lane, w, swapped)
        wdup[1, p] = jnp.where(near_lane, swapped, w)

    b_load.wait()
    turn_d = iota((XM, XM), 0) - iota((XM, XM), 1)
    turn_by = lax.rem(starts[me], ALIGN)
    turn = (turn_d == turn_by) | (turn_d == turn_by - XM)
    turned = mm(one_hot(turn), bwd[...]).astype(BF16)
    turned = jnp.concatenate([turned[:, :XM], turned[:, XM:]], axis=0)

    q_load.wait()
    column = iota((nf, xa), 0)
    at_row = jnp.zeros((nf, xa), jnp.int32)
    at_row = lax.fori_loop(0, nf, lambda j, v: jnp.where(column == j, fac[j], v), at_row)
    picks = one_hot(iota((nf, xa), 1) == at_row)
    unit = math.sqrt(nf * XM) * image_gain(nf, xa)
    shifts[0] = mm(picks, qv[:xa]) * unit
    shifts[1] = mm(picks, qv[xa:]) * -unit
    with_re = mm(turned, qv[:XM])
    with_im = mm(turned, qv[xa : xa + XM])
    base_re = with_re[:XM] + with_im[XM:]
    base_im = with_re[XM:] - with_im[:XM]

    def back_table(j):
        re, im = shifts[0, pl.ds(j, 1), :], shifts[1, pl.ds(j, 1), :]
        ctab[j, :XM] = (base_re * re - base_im * im).astype(BF16)
        ctab[j, XM:] = (base_re * im + base_im * re).astype(BF16)

    each(0, nf, back_table)

    sent(send1.at[0, pl.ds(0, nf - 1)], s1.at[0])
    each_down(near, nf, lambda i: send_first(1, i, 1).start())
    each_down(1, near, lambda i: send_first(1, i, 0).start())

    def twist(prod):
        n = prod.shape[0] // 2
        crossed = pltpu.roll(prod[n:], half, 1)
        first = iota(crossed.shape, 1) < half
        return prod[:n] + jnp.where(first, -crossed, crossed)

    def arrived(h, first, last):
        return recv1[h, first:last].reshape((last - first) * XM, width)

    for h in range(2):
        near_blocks, far_blocks = recv1.at[h, pl.ds(0, near - 1)], recv1.at[h, pl.ds(0, nf - near)]
        if folded:
            split = near * XM
            received(near_blocks, r1.at[h, 0])
            acc[...] = mm(places[:, :split], arrived(h, 0, near))
            received(far_blocks, r1.at[h, 1])
            acc[...] += mm(places[:, split:], arrived(h, near, nf))
        else:
            acc[...] = mm(hit(grid_d, me), recv1[h, 0])

            def gather(i):
                acc[...] += mm(hit(grid_d, source(i)), recv1[h, i])

            received(near_blocks, r1.at[h, 0])
            each(1, near, gather)
            received(far_blocks, r1.at[h, 1])
            each(near, nf, gather)
        prod = mm(qv[...], acc[...].astype(BF16))
        spectrum = twist(prod)
        crossed = wdup[h, 1] * pltpu.roll(spectrum, half, 1)
        weighted = wdup[h, 0] * spectrum + jnp.where(near_lane, -crossed, crossed)
        weighted = weighted.astype(BF16)

        def back(j):
            return twist(mm(ctab[j], weighted)).astype(BF16)

        terms[c, me, h] = back(me)
        for q in range(1, nx):
            forward_x(h, 0, q, 0).start()
        forward_partner(c, h, 0, 0).start()

        def second(i, far):
            j = peer(i)
            send2[h, j] = back(j)
            send_second(h, i, far).start()

        def second_near(i):
            second(i, 0)
            for q in range(1, nx):
                send_direct(h, i, q).start()

        each(1, near, second_near)
        each(near, nf, lambda i: second(i, 1))
        if h == 0:
            window_maps()

    sent(sall.at[pl.ds(0, ncol - 1)], ss.at[0])
    received(sall.at[pl.ds(0, ncol - 1)], rs.at[0])
    starts_copy = pltpu.make_async_copy(sall, starts_out, ld.at[9])
    starts_copy.start()

    def relay_near(h):
        received(terms.at[0, pl.ds(0, near - 1), h], ro_near.at[h])
        each(1, near, lambda i: forward_partner(c, h, i, 0).start())

    def relay_across_near(h):
        for q in range(1, nx):
            received(terms.at[0, pl.ds(0, near), h], rx_near.at[q - 1, h])
            each(0, near, lambda i: forward_partner(behind[q], h, i, 0).start())

    def relay_far(i, h):
        received(terms.at[c, source(i), h], own_arrival(h, i, 1))
        for q in range(1, nx):
            forward_x(h, i, q, 1).start()
        forward_partner(c, h, i, 1).start()

    def relay_across(i, h):
        for q in range(1, nx):
            received(terms.at[behind[q], source(i), h], across_arrival(h, i, q, 1))
            forward_partner(behind[q], h, i, 1).start()

    def relay_both(i):
        relay_far(i, 1)
        relay_across(i, 0)

    def map_near(i):
        j = source(i)
        for k in range(ncol):
            values[k, i] = mm(jnp.concatenate([terms[k, j, 0], terms[k, j, 1]], axis=1), maps[k])

    each(near, nf, lambda i: relay_far(i, 0))
    relay_near(0)
    relay_near(1)
    relay_across_near(0)
    relay_across_near(1)
    received(terms.at[pl.ds(0, nx), pl.ds(0, near)], rp.at[0])
    def relay_map(i):
        relay_both(i)
        if early:
            map_near(i - near)

    each(near, nf, relay_map)
    each(near, nf, lambda i: relay_across(i, 1))
    for h in range(2):
        received(terms.at[pl.ds(0, nx), pl.ds(0, nf - near), h], rp.at[1 + h])

    starts_copy.wait()
    for h in range(2):
        if h:
            sent(send1.at[h, pl.ds(0, nf - 1)], s1.at[h])
        sent(send2.at[h, pl.ds(0, nf - 1)], s2.at[h])
        sent(terms.at[pl.ds(0, nx), :, h], sp.at[h])
        for q in range(1, nx):
            sent(terms.at[0, pl.ds(0, near - 1), h], sd.at[q - 1, h])
            sent(terms.at[0, pl.ds(0, nf - near + 1), h], sx.at[q - 1, h])


def image_gain(nf, xa):
    return math.sqrt(nf * XM) / math.sqrt(xa)


def finish_kernel(nf, ncol, near, early, starts_all, terms, values, maps, out, acc, stage, seen, code, osem):
    me = lax.axis_index("facet")
    c = lax.axis_index("col")
    own_rows = out.shape[1]
    oc = out.shape[2]
    total = own_rows * ncol
    base = c * own_rows
    pow2 = nf & (nf - 1) == 0

    def source(i):
        if not pow2:
            return lax.rem(me + nf - i, nf)
        return jnp.bitwise_xor(me, i)

    acc[...] = jnp.zeros_like(acc)
    slot = iota((XM, 2 * oc), 0)
    edge = iota((ALIGN, 2 * oc), 0)

    split = near if early else 0
    mid = XM + own_rows // 2

    def listed(kind, first, last):
        def note(cc, i, counts):
            upper, lower = counts
            j = source(i)
            rel = starts_all[cc, 0, j] - base
            rel = jnp.where(rel < 0, rel + total, rel)
            rel = jnp.where(rel >= total - XM, rel - total, rel) + XM
            inside = rel < own_rows + XM
            is_lower = rel >= mid
            spot = jnp.where(is_lower, lower, upper)
            place = jnp.where(is_lower, 1, 0)
            seen[kind, place, spot] = rel
            code[kind, place, spot] = i * ncol + cc
            one = jnp.where(inside, 1, 0)
            return upper + one * (1 - place), lower + one * place

        zero = jnp.int32(0)
        counts = (zero, zero)
        for cc in range(ncol):
            if nf <= 8:
                for i in range(first, last):
                    counts = note(cc, i, counts)
            else:
                counts = lax.fori_loop(first, last, lambda i, n: note(cc, i, n), counts)
        return counts

    def gather(kind, place, count, value_of):
        @pl.loop(0, count)
        def _(t):
            rel, term = seen[kind, place, t], code[kind, place, t]
            i = lax.div(term, ncol)
            cc = term - i * ncol
            value = value_of(cc, i, source(i))
            turn = jnp.bitwise_and(rel, ALIGN - 1)
            low = pl.multiple_of(rel - turn, ALIGN)
            acc[pl.ds(low, XM), :] += jnp.where(slot >= turn, value, 0.0)
            acc[pl.ds(pl.multiple_of(low + XM, ALIGN), ALIGN), :] += jnp.where(
                edge < turn, value[:ALIGN], 0.0
            )

    def mapped(cc, i, j):
        return mm(jnp.concatenate([terms[cc, j, 0], terms[cc, j, 1]], axis=1), maps[cc])

    early_counts = listed(0, 0, split) if early else None
    late_counts = listed(1, split, nf)
    chunk = own_rows // OUT_CHUNKS
    for place in range(2):
        if early:
            gather(0, place, early_counts[place], lambda cc, i, j: values[cc, i])
        gather(1, place, late_counts[place], mapped)
        for k in range(place * OUT_CHUNKS // 2, (place + 1) * OUT_CHUNKS // 2):
            rows = pl.ds(k * chunk, chunk)
            src = pl.ds(XM + k * chunk, chunk)
            stage[0, rows, :] = acc[src, :oc].astype(BF16)
            stage[1, rows, :] = acc[src, oc:].astype(BF16)
            pltpu.make_async_copy(stage.at[:, rows, :], out.at[:, rows, :], osem.at[0]).start()
    pltpu.make_async_copy(stage, out, osem.at[0]).wait()


def body(prepared, sub_off, fac_off, win_col, vis_weights):
    nf = fac_off.shape[0]
    ncol = lax.axis_size("col")
    facet_strip = prepared[0]
    facet_len, width = facet_strip.shape[1:]
    strip_blocks = facet_strip.reshape(2, facet_len // XM, XM, width)
    weights = vis_weights[0]
    xa = weights.shape[1]
    oc = width * ncol // 2
    own_rows = facet_len // ncol
    starts = sub_off[:, 0]
    lanes = -(-nf // 128) * 128
    near = nf // 2 if nf & (nf - 1) == 0 else 1
    nx = ncol // 2
    early = ncol * near * XM * 2 * oc * 4 <= TABLE_LIMIT
    folded = xa * nf * XM * 2 <= TABLE_LIMIT // 4

    forward, backward = window_tables(XM)
    q_table = stacked(*dft(xa, -1.0, 1.0 / math.sqrt(nf * XM)), 0)
    out_map = stacked(*dft(oc, 1.0, 1.0 / math.sqrt(2 * oc)), 1)

    smem = pl.BlockSpec(memory_space=pltpu.SMEM)
    vmem = pl.BlockSpec(memory_space=pltpu.VMEM)
    hbm = pl.BlockSpec(memory_space=pl.ANY)
    dma = pltpu.SemaphoreType.DMA
    halves = pltpu.VMEM((2, nf, XM, width), BF16)
    operands = (
        starts, fac_off, strip_blocks, weights, jnp.asarray(forward), jnp.asarray(backward),
        win_col, jnp.asarray(out_map), jnp.asarray(q_table),
    )
    held = (ncol, near, XM, 2 * oc) if early else (8, 128)
    results = pl.pallas_call(
        functools.partial(exchange_kernel, nf, ncol, near, early, folded),
        out_shape=(
            pltpu.VMEM((ncol, nf, 2, XM, width), BF16),
            pltpu.VMEM(held, F32),
            pltpu.VMEM((ncol, 2 * width, 2 * oc), BF16),
            pltpu.SMEM((ncol, 8, lanes), jnp.int32),
        ),
        in_specs=[hbm] * len(operands),
        out_specs=(vmem, vmem, vmem, smem),
        scratch_shapes=[
            pltpu.SMEM((nf,), jnp.int32),
            pltpu.SMEM((nf,), jnp.int32),
            pltpu.VMEM(forward.shape, BF16),
            pltpu.VMEM(backward.shape, BF16),
            pltpu.VMEM(win_col.shape, jnp.int32),
            pltpu.VMEM(strip_blocks.shape, BF16),
            pltpu.VMEM(q_table.shape, BF16),
            pltpu.VMEM(weights.shape, BF16),
            halves,
            halves,
            pltpu.VMEM((xa, width), F32),
            halves,
            pltpu.VMEM((xa, nf * XM) if folded else (8, 128), BF16),
            pltpu.VMEM((2, nf, xa), F32),
            pltpu.VMEM((nf, 2 * XM, xa), BF16),
            pltpu.VMEM((8, lanes), jnp.int32),
            pltpu.VMEM((ncol, 8, lanes), jnp.int32),
            pltpu.VMEM(out_map.shape, BF16),
            pltpu.VMEM((2, 2, xa, width), F32),
            dma((10,)), dma((2,)), dma((2, 2)), dma((2,)),
            dma((nx - 1, 2)), dma((nx - 1, 2)), dma((2,)),
            dma((2,)), dma((2, nf - near)), dma((nx - 1, 2)), dma((nx - 1, 2, nf - near)), dma((3,)),
            dma((1,)), dma((1,)),
        ],
        compiler_params=pltpu.CompilerParams(
            collective_id=0, has_side_effects=True, vmem_limit_bytes=VMEM_LIMIT
        ),
        name="exchange",
    )(*[pltpu.with_memory_space_constraint(x, pltpu.HBM) for x in operands])
    terms, values, maps, starts_all = results
    spaces = (pltpu.SMEM, pltpu.VMEM, pltpu.VMEM, pltpu.VMEM)
    out = pl.pallas_call(
        functools.partial(finish_kernel, nf, ncol, near, early),
        out_shape=jax.ShapeDtypeStruct((2, own_rows, oc), BF16),
        in_specs=[smem, vmem, vmem, vmem],
        out_specs=hbm,
        scratch_shapes=[
            pltpu.VMEM((own_rows + 2 * XM + ALIGN, 2 * oc), F32),
            pltpu.VMEM((2, own_rows, oc), BF16),
            pltpu.SMEM((2, 2, ncol * nf + 1), jnp.int32),
            pltpu.SMEM((2, 2, ncol * nf + 1), jnp.int32),
            dma((1,)),
        ],
        compiler_params=pltpu.CompilerParams(vmem_limit_bytes=VMEM_LIMIT),
        name="finish",
    )(*[pltpu.with_memory_space_constraint(x, m) for x, m in zip((starts_all, terms, values, maps), spaces)])
    return out[None]


def solution(mesh):
    in_specs = (
        P("facet", None, None, "col"),
        P(None, "col"),
        P(),
        P(),
        P("facet", None, None, "col"),
    )
    out_specs = P("facet", None, "col", None)
    return jax.shard_map(body, mesh=mesh, in_specs=in_specs, out_specs=out_specs, check_vma=False)
```

```python
import functools
import math

import jax
import jax.numpy as jnp
import numpy as np
from jax import lax
from jax.experimental import pallas as pl
from jax.experimental.pallas import tpu as pltpu
from jax.sharding import PartitionSpec as P

XM = 128
ALIGN = 16
OUT_CHUNKS = 8
GROUP = 3
TABLE_LIMIT = 16 * 2**20
VMEM_LIMIT = 40 * 2**20
MESH = pl.DeviceIdType.MESH
F32 = jnp.float32
BF16 = jnp.bfloat16


def dft(length, sign, scaling):
    ids = np.arange(length)
    angles = 2.0 * np.pi / length * (ids[:, None] * ids[None, :] % length)
    return np.cos(angles) * scaling, sign * np.sin(angles) * scaling


def stacked(real_part, imag_part, axis):
    return np.concatenate([real_part, imag_part], axis=axis).astype(jnp.bfloat16)


def window_tables(length):
    taper = 0.3 + 0.7 * np.sin(np.pi * (np.arange(length) + 0.5) / length) ** 2
    scaling = 1.0 / math.sqrt(length)
    fwd_re, fwd_im = dft(length, -1.0, scaling)
    back_re, back_im = dft(length, 1.0, scaling)
    forward = stacked(fwd_re * taper[None, :], fwd_im * taper[None, :], 0)
    backward = stacked(back_re * taper[:, None], back_im * taper[:, None], 1)
    return forward, backward


def mm(a, b):
    return jnp.dot(a, b, preferred_element_type=F32)


def iota(shape, dim):
    return lax.broadcasted_iota(jnp.int32, shape, dim)


def one_hot(hit):
    return jnp.where(hit, 1.0, 0.0).astype(BF16)


def exchange_kernel(
    nf, ncol, near, early, folded, starts_in, fac_in, prep, wts, fwd_in, bwd_in, win_in, fmap, qtab,
    terms, values, maps, starts_out,
    starts, fac, fwd, bwd, win, pv, qv, wv, send1, recv1, acc, send2, places, shifts, ctab, svec, sall, fv, wdup,
    ld, s1, r1, s2, sd, sx, sp, ro_near, ro_far, rx_near, rx_far, rp, ss, rs,
):
    me = lax.axis_index("facet")
    c = lax.axis_index("col")
    nx = ncol // 2
    xq, core = lax.div(c, 2), lax.rem(c, 2)
    partner = xq * 2 + 1 - core
    pow2 = nf & (nf - 1) == 0
    blocks = prep.shape[1]
    xa, width = wts.shape[1:]
    half = width // 2
    oc = fmap.shape[0]
    deep = nf <= 8
    middle = (near + nf) // 2

    bits = [1 << b for b in range((nf - 1).bit_length())] if pow2 else []
    flips = [b - 2 * b * lax.rem(lax.div(me, b), 2) for b in bits]
    across = [lax.rem(xq + q, nx) * 2 + core for q in range(nx)]
    behind = [lax.rem(xq + nx - q, nx) * 2 + core for q in range(nx)]

    def peer(i):
        if not pow2:
            return lax.rem(me + i, nf)
        out = me
        for b, flip in zip(bits, flips):
            if isinstance(i, int):
                out = out + flip if i & b else out
            else:
                out = out + flip * lax.rem(lax.div(i, b), 2)
        return out

    def source(i):
        return peer(i) if pow2 else lax.rem(me + nf - i, nf)

    def each(first, last, step):
        if not deep:
            pl.loop(first, last)(step)
            return
        for i in range(first, last):
            step(i)

    def each_down(first, last, step):
        each(0, last - first, lambda k: step(last - 1 - k))

    barrier = pltpu.get_barrier_semaphore()

    def greet(i):
        pl.semaphore_signal(barrier, inc=1, device_id={"facet": peer(i)}, device_id_type=MESH)

    each(1, nf, greet)

    for i in range(1, ncol):
        pl.semaphore_signal(
            barrier, inc=1, device_id={"col": lax.rem(c + i, ncol)}, device_id_type=MESH
        )

    def greet_across(i):
        for q in range(1, nx):
            pl.semaphore_signal(
                barrier, inc=1, device_id={"facet": peer(i), "col": across[q]}, device_id_type=MESH
            )

    each(1, near, greet_across)

    strip_load = pltpu.make_async_copy(prep, pv, ld.at[0])
    small = [(starts_in, starts), (fac_in, fac), (fwd_in, fwd)]
    later = [(win_in, win), (fmap, fv), (bwd_in, bwd), (wts, wv), (qtab, qv)]
    small = [pltpu.make_async_copy(*pair, ld.at[1 + k]) for k, pair in enumerate(small)]
    later = [pltpu.make_async_copy(*pair, ld.at[4 + k]) for k, pair in enumerate(later)]
    for copy in [*small, strip_load, *later]:
        copy.start()
    win_load, f_load, b_load, w_load, q_load = later
    for copy in small:
        copy.wait()

    lane = iota(svec.shape, 1)
    row = jnp.zeros(svec.shape, jnp.int32)
    svec[...] = lax.fori_loop(0, nf, lambda j, v: jnp.where(lane == j, starts[j], v), row)

    def remote(src, dst, send, recv, **where):
        return pltpu.make_async_remote_copy(
            src_ref=src, dst_ref=dst, send_sem=send, recv_sem=recv,
            device_id=where, device_id_type=MESH,
        )

    def send_first(h, i, far):
        j = peer(i)
        return remote(send1.at[h, j], recv1.at[h, i], s1.at[h], r1.at[h, far], facet=j)

    def own_arrival(h, i, far):
        return ro_far.at[h, i - near] if far else ro_near.at[h]

    def across_arrival(h, i, q, far):
        return rx_far.at[q - 1, h, i - near] if far else rx_near.at[q - 1, h]

    def send_second(h, i, far):
        j = peer(i)
        arrived = own_arrival(h, i, far)
        return remote(send2.at[h, j], terms.at[c, me, h], s2.at[h], arrived, facet=j)

    def send_direct(h, i, q):
        j = peer(i)
        return remote(
            send2.at[h, j], terms.at[c, me, h], sd.at[q - 1, h], across_arrival(h, i, q, 0),
            facet=j, col=across[q],
        )

    def forward_x(h, i, q, far):
        block = terms.at[c, source(i), h]
        arrived = across_arrival(h, i, q, far)
        return remote(block, block, sx.at[q - 1, h], arrived, col=across[q])

    def forward_partner(cc, h, i, far):
        block = terms.at[cc, source(i), h]
        return remote(block, block, sp.at[h], rp.at[far * (1 + h)], col=partner)

    def sent(block, sem):
        remote(block, block, sem, rs.at[0], col=partner).wait_send()

    def received(block, sem):
        remote(block, block, ss.at[0], sem, col=partner).wait_recv()

    row_d = iota((XM, 2 * XM), 1) - iota((XM, 2 * XM), 0)
    fwd_table = fwd[...]

    def contribution(j, dst, at):
        start = starts[j]
        block = lax.div(start, XM)
        shift = start - block * XM
        above = jnp.where(block + 1 == blocks, 0, block + 1)
        top = jnp.concatenate([pv[0, block], pv[1, block]], axis=1)
        low = jnp.concatenate([pv[0, above], pv[1, above]], axis=1)
        picked = mm(one_hot(row_d == shift), jnp.concatenate([top, low], axis=0))
        prod = mm(fwd_table, picked.astype(BF16))
        re = prod[:XM, :width] - prod[XM:, width:]
        im = prod[:XM, width:] + prod[XM:, :width]
        first = iota(re.shape, 1) < half
        dst[0, at] = jnp.where(first, re, pltpu.roll(im, half, 1)).astype(BF16)
        dst[1, at] = jnp.where(first, pltpu.roll(re, half, 1), im).astype(BF16)

    def window_maps():
        win_load.wait()
        f_load.wait()
        fm = fv[...]
        col_n = iota((oc, width), 0)
        for k in range(ncol):
            m = lax.dot_general(
                one_hot(col_n == win[k : k + 1, :]), fm, (((0,), (0,)), ((), ())),
                preferred_element_type=F32,
            ).astype(BF16)
            m_re, m_im = m[:, :oc], m[:, oc:]
            upper = jnp.concatenate([m_re, m_im], axis=1)
            lower = jnp.concatenate([-m_im, m_re], axis=1)
            maps[k] = jnp.concatenate(
                [upper[:half], lower[:half], upper[half:], lower[half:]], axis=0
            )

    strip_load.wait()
    pl.semaphore_wait(barrier, nf - 1 + ncol - 1 + (near - 1) * (nx - 1))

    def first(i, far):
        contribution(peer(i), send1, peer(i))
        send_first(0, i, far).start()

    each_down(near, nf, lambda i: first(i, 1))
    each_down(1, near, lambda i: first(i, 0))

    contribution(me, recv1, 0)

    for i in range(1, ncol):
        to = lax.rem(c + i, ncol)
        remote(svec, sall.at[c], ss.at[0], rs.at[0], col=to).start()
    sall[c] = svec[...]

    grid_d = iota((xa, XM), 0) - iota((xa, XM), 1)
    back_d = iota((XM, xa), 1) - iota((XM, xa), 0)

    def hit(diff, j):
        return one_hot((diff == fac[j]) | (diff == fac[j] - xa))

    if folded:
        for i in range(nf):
            places[:, i * XM : (i + 1) * XM] = hit(grid_d, source(i))

    w_load.wait()
    near_lane = iota((xa, width), 1) < half
    for p in range(2):
        w = wv[p].astype(F32)
        swapped = pltpu.roll(w, half, 1)
        wdup[0, p] = jnp.where(near_lane, w, swapped)
        wdup[1, p] = jnp.where(near_lane, swapped, w)

    b_load.wait()
    turn_d = iota((XM, XM), 0) - iota((XM, XM), 1)
    turn_by = lax.rem(starts[me], ALIGN)
    turn = (turn_d == turn_by) | (turn_d == turn_by - XM)
    turned = mm(one_hot(turn), bwd[...]).astype(BF16)
    turned = jnp.concatenate([turned[:, :XM], turned[:, XM:]], axis=0)

    q_load.wait()
    column = iota((nf, xa), 0)
    at_row = jnp.zeros((nf, xa), jnp.int32)
    at_row = lax.fori_loop(0, nf, lambda j, v: jnp.where(column == j, fac[j], v), at_row)
    picks = one_hot(iota((nf, xa), 1) == at_row)
    unit = math.sqrt(nf * XM) * image_gain(nf, xa)
    shifts[0] = mm(picks, qv[:xa]) * unit
    shifts[1] = mm(picks, qv[xa:]) * -unit
    with_re = mm(turned, qv[:XM])
    with_im = mm(turned, qv[xa : xa + XM])
    base_re = with_re[:XM] + with_im[XM:]
    base_im = with_re[XM:] - with_im[:XM]

    def back_table(j):
        re, im = shifts[0, pl.ds(j, 1), :], shifts[1, pl.ds(j, 1), :]
        ctab[j, :XM] = (base_re * re - base_im * im).astype(BF16)
        ctab[j, XM:] = (base_re * im + base_im * re).astype(BF16)

    each(0, nf, back_table)

    sent(send1.at[0, pl.ds(0, nf - 1)], s1.at[0])
    each_down(near, nf, lambda i: send_first(1, i, 1).start())
    each_down(1, near, lambda i: send_first(1, i, 0).start())

    def twist(prod):
        n = prod.shape[0] // 2
        crossed = pltpu.roll(prod[n:], half, 1)
        first = iota(crossed.shape, 1) < half
        return prod[:n] + jnp.where(first, -crossed, crossed)

    def arrived(h, first, last):
        return recv1[h, first:last].reshape((last - first) * XM, width)

    for h in range(2):
        near_blocks, far_blocks = recv1.at[h, pl.ds(0, near - 1)], recv1.at[h, pl.ds(0, nf - near)]
        if folded:
            split = near * XM
            received(near_blocks, r1.at[h, 0])
            acc[...] = mm(places[:, :split], arrived(h, 0, near))
            received(far_blocks, r1.at[h, 1])
            acc[...] += mm(places[:, split:], arrived(h, near, nf))
        else:
            acc[...] = mm(hit(grid_d, me), recv1[h, 0])

            def gather(i):
                acc[...] += mm(hit(grid_d, source(i)), recv1[h, i])

            received(near_blocks, r1.at[h, 0])
            each(1, near, gather)
            received(far_blocks, r1.at[h, 1])
            each(near, nf, gather)
        prod = mm(qv[...], acc[...].astype(BF16))
        spectrum = twist(prod)
        crossed = wdup[h, 1] * pltpu.roll(spectrum, half, 1)
        weighted = wdup[h, 0] * spectrum + jnp.where(near_lane, -crossed, crossed)
        weighted = weighted.astype(BF16)

        def back(j):
            return twist(mm(ctab[j], weighted)).astype(BF16)

        terms[c, me, h] = back(me)
        for q in range(1, nx):
            forward_x(h, 0, q, 0).start()
        forward_partner(c, h, 0, 0).start()

        def second(i, far, late=False):
            j = peer(i)
            send2[h, j] = back(j)
            if not (h and late):
                send_second(h, i, far).start()

        def second_near(i):
            second(i, 0)
            for q in range(1, nx):
                send_direct(h, i, q).start()

        each(1, near, second_near)
        each(near, middle, lambda i: second(i, 1))
        each(middle, nf, lambda i: second(i, 1, True))
        if h == 0:
            window_maps()

    sent(sall.at[pl.ds(0, ncol - 1)], ss.at[0])
    received(sall.at[pl.ds(0, ncol - 1)], rs.at[0])
    starts_copy = pltpu.make_async_copy(sall, starts_out, ld.at[9])
    starts_copy.start()

    def relay_near(h):
        received(terms.at[0, pl.ds(0, near - 1), h], ro_near.at[h])
        each(1, near, lambda i: forward_partner(c, h, i, 0).start())

    def relay_across_near(h):
        for q in range(1, nx):
            received(terms.at[0, pl.ds(0, near), h], rx_near.at[q - 1, h])
            each(0, near, lambda i: forward_partner(behind[q], h, i, 0).start())

    def relay_far(i, h):
        received(terms.at[c, source(i), h], own_arrival(h, i, 1))
        for q in range(1, nx):
            forward_x(h, i, q, 1).start()
        forward_partner(c, h, i, 1).start()

    def relay_across(i, h):
        for q in range(1, nx):
            received(terms.at[behind[q], source(i), h], across_arrival(h, i, q, 1))
            forward_partner(behind[q], h, i, 1).start()

    def relay_both(i):
        relay_far(i, 1)
        relay_across(i, 0)

    def map_near(i):
        j = source(i)
        for k in range(ncol):
            values[k, i] = mm(jnp.concatenate([terms[k, j, 0], terms[k, j, 1]], axis=1), maps[k])

    each(near, near + 1, lambda i: relay_far(i, 0))
    each(middle, nf, lambda i: send_second(1, i, 1).start())
    each(near + 1, nf, lambda i: relay_far(i, 0))
    relay_near(0)
    relay_near(1)
    relay_across_near(0)
    relay_across_near(1)
    received(terms.at[pl.ds(0, nx), pl.ds(0, near)], rp.at[0])
    def relay_map(i):
        relay_both(i)
        if early:
            map_near(i - near)

    each(near, nf, relay_map)
    each(near, nf, lambda i: relay_across(i, 1))
    for h in range(2):
        received(terms.at[pl.ds(0, nx), pl.ds(0, nf - near), h], rp.at[1 + h])

    starts_copy.wait()
    for h in range(2):
        if h:
            sent(send1.at[h, pl.ds(0, nf - 1)], s1.at[h])
        sent(send2.at[h, pl.ds(0, nf - 1)], s2.at[h])
        sent(terms.at[pl.ds(0, nx), :, h], sp.at[h])
        for q in range(1, nx):
            sent(terms.at[0, pl.ds(0, near - 1), h], sd.at[q - 1, h])
            sent(terms.at[0, pl.ds(0, nf - near + 1), h], sx.at[q - 1, h])


def image_gain(nf, xa):
    return math.sqrt(nf * XM) / math.sqrt(xa)


def finish_kernel(nf, ncol, near, early, starts_all, terms, values, maps, out, acc, stage, seen, code, osem):
    me = lax.axis_index("facet")
    c = lax.axis_index("col")
    own_rows = out.shape[1]
    oc = out.shape[2]
    total = own_rows * ncol
    base = c * own_rows
    pow2 = nf & (nf - 1) == 0

    def source(i):
        if not pow2:
            return lax.rem(me + nf - i, nf)
        return jnp.bitwise_xor(me, i)

    acc[...] = jnp.zeros_like(acc)
    slot = iota((XM, 2 * oc), 0)
    edge = iota((ALIGN, 2 * oc), 0)

    split = near if early else 0
    mid = XM + own_rows // 2

    def listed(kind, first, last):
        def note(cc, i, counts):
            upper, lower = counts
            j = source(i)
            rel = starts_all[cc, 0, j] - base
            rel = jnp.where(rel < 0, rel + total, rel)
            rel = jnp.where(rel >= total - XM, rel - total, rel) + XM
            inside = rel < own_rows + XM
            is_lower = rel >= mid
            spot = jnp.where(is_lower, lower, upper)
            place = jnp.where(is_lower, 1, 0)
            seen[kind, place, spot] = rel
            code[kind, place, spot] = i * ncol + cc
            one = jnp.where(inside, 1, 0)
            return upper + one * (1 - place), lower + one * place

        zero = jnp.int32(0)
        counts = (zero, zero)
        for cc in range(ncol):
            if nf <= 8:
                for i in range(first, last):
                    counts = note(cc, i, counts)
            else:
                counts = lax.fori_loop(first, last, lambda i, n: note(cc, i, n), counts)
        for place in range(2):
            for k in range(GROUP - 1):
                seen[kind, place, counts[place] + k] = 0
                code[kind, place, counts[place] + k] = first * ncol
        return counts

    def gather(kind, place, count, value_of):
        def load(t):
            term = code[kind, place, t]
            i = lax.div(term, ncol)
            return seen[kind, place, t], value_of(term - i * ncol, i, source(i))

        def add(rel, value):
            turn = jnp.bitwise_and(rel, ALIGN - 1)
            low = pl.multiple_of(rel - turn, ALIGN)
            acc[pl.ds(low, XM), :] += jnp.where(slot >= turn, value, 0.0)
            acc[pl.ds(pl.multiple_of(low + XM, ALIGN), ALIGN), :] += jnp.where(
                edge < turn, value[:ALIGN], 0.0
            )

        @pl.loop(0, lax.div(count + GROUP - 1, GROUP))
        def _(t):
            pairs = [load(t * GROUP + k) for k in range(GROUP)]
            for rel, value in pairs:
                add(rel, value)

    def mapped(cc, i, j):
        return mm(jnp.concatenate([terms[cc, j, 0], terms[cc, j, 1]], axis=1), maps[cc])

    early_counts = listed(0, 0, split) if early else None
    late_counts = listed(1, split, nf)
    chunk = own_rows // OUT_CHUNKS
    for place in range(2):
        if early:
            gather(0, place, early_counts[place], lambda cc, i, j: values[cc, i])
        gather(1, place, late_counts[place], mapped)
        for k in range(place * OUT_CHUNKS // 2, (place + 1) * OUT_CHUNKS // 2):
            rows = pl.ds(k * chunk, chunk)
            src = pl.ds(XM + k * chunk, chunk)
            stage[0, rows, :] = acc[src, :oc].astype(BF16)
            stage[1, rows, :] = acc[src, oc:].astype(BF16)
            pltpu.make_async_copy(stage.at[:, rows, :], out.at[:, rows, :], osem.at[0]).start()
    pltpu.make_async_copy(stage, out, osem.at[0]).wait()


def body(prepared, sub_off, fac_off, win_col, vis_weights):
    nf = fac_off.shape[0]
    ncol = lax.axis_size("col")
    facet_strip = prepared[0]
    facet_len, width = facet_strip.shape[1:]
    strip_blocks = facet_strip.reshape(2, facet_len // XM, XM, width)
    weights = vis_weights[0]
    xa = weights.shape[1]
    oc = width * ncol // 2
    own_rows = facet_len // ncol
    starts = sub_off[:, 0]
    lanes = -(-nf // 128) * 128
    near = nf // 2 if nf & (nf - 1) == 0 else 1
    nx = ncol // 2
    early = ncol * near * XM * 2 * oc * 4 <= TABLE_LIMIT
    folded = xa * nf * XM * 2 <= TABLE_LIMIT // 4

    forward, backward = window_tables(XM)
    q_table = stacked(*dft(xa, -1.0, 1.0 / math.sqrt(nf * XM)), 0)
    out_map = stacked(*dft(oc, 1.0, 1.0 / math.sqrt(2 * oc)), 1)

    smem = pl.BlockSpec(memory_space=pltpu.SMEM)
    vmem = pl.BlockSpec(memory_space=pltpu.VMEM)
    hbm = pl.BlockSpec(memory_space=pl.ANY)
    dma = pltpu.SemaphoreType.DMA
    halves = pltpu.VMEM((2, nf, XM, width), BF16)
    operands = (
        starts, fac_off, strip_blocks, weights, jnp.asarray(forward), jnp.asarray(backward),
        win_col, jnp.asarray(out_map), jnp.asarray(q_table),
    )
    held = (ncol, near, XM, 2 * oc) if early else (8, 128)
    results = pl.pallas_call(
        functools.partial(exchange_kernel, nf, ncol, near, early, folded),
        out_shape=(
            pltpu.VMEM((ncol, nf, 2, XM, width), BF16),
            pltpu.VMEM(held, F32),
            pltpu.VMEM((ncol, 2 * width, 2 * oc), BF16),
            pltpu.SMEM((ncol, 8, lanes), jnp.int32),
        ),
        in_specs=[hbm] * len(operands),
        out_specs=(vmem, vmem, vmem, smem),
        scratch_shapes=[
            pltpu.SMEM((nf,), jnp.int32),
            pltpu.SMEM((nf,), jnp.int32),
            pltpu.VMEM(forward.shape, BF16),
            pltpu.VMEM(backward.shape, BF16),
            pltpu.VMEM(win_col.shape, jnp.int32),
            pltpu.VMEM(strip_blocks.shape, BF16),
            pltpu.VMEM(q_table.shape, BF16),
            pltpu.VMEM(weights.shape, BF16),
            halves,
            halves,
            pltpu.VMEM((xa, width), F32),
            halves,
            pltpu.VMEM((xa, nf * XM) if folded else (8, 128), BF16),
            pltpu.VMEM((2, nf, xa), F32),
            pltpu.VMEM((nf, 2 * XM, xa), BF16),
            pltpu.VMEM((8, lanes), jnp.int32),
            pltpu.VMEM((ncol, 8, lanes), jnp.int32),
            pltpu.VMEM(out_map.shape, BF16),
            pltpu.VMEM((2, 2, xa, width), F32),
            dma((10,)), dma((2,)), dma((2, 2)), dma((2,)),
            dma((nx - 1, 2)), dma((nx - 1, 2)), dma((2,)),
            dma((2,)), dma((2, nf - near)), dma((nx - 1, 2)), dma((nx - 1, 2, nf - near)), dma((3,)),
            dma((1,)), dma((1,)),
        ],
        compiler_params=pltpu.CompilerParams(
            collective_id=0, has_side_effects=True, vmem_limit_bytes=VMEM_LIMIT
        ),
        name="exchange",
    )(*[pltpu.with_memory_space_constraint(x, pltpu.HBM) for x in operands])
    terms, values, maps, starts_all = results
    spaces = (pltpu.SMEM, pltpu.VMEM, pltpu.VMEM, pltpu.VMEM)
    out = pl.pallas_call(
        functools.partial(finish_kernel, nf, ncol, near, early),
        out_shape=jax.ShapeDtypeStruct((2, own_rows, oc), BF16),
        in_specs=[smem, vmem, vmem, vmem],
        out_specs=hbm,
        scratch_shapes=[
            pltpu.VMEM((own_rows + 2 * XM + ALIGN, 2 * oc), F32),
            pltpu.VMEM((2, own_rows, oc), BF16),
            pltpu.SMEM((2, 2, ncol * nf + GROUP), jnp.int32),
            pltpu.SMEM((2, 2, ncol * nf + GROUP), jnp.int32),
            dma((1,)),
        ],
        compiler_params=pltpu.CompilerParams(vmem_limit_bytes=VMEM_LIMIT),
        name="finish",
    )(*[pltpu.with_memory_space_constraint(x, m) for x, m in zip((starts_all, terms, values, maps), spaces)])
    return out[None]


def solution(mesh):
    in_specs = (
        P("facet", None, None, "col"),
        P(None, "col"),
        P(),
        P(),
        P("facet", None, None, "col"),
    )
    out_specs = P("facet", None, "col", None)
    return jax.shard_map(body, mesh=mesh, in_specs=in_specs, out_specs=out_specs, check_vma=False)
```

```python
import functools
import math

import jax
import jax.numpy as jnp
import numpy as np
from jax import lax
from jax.experimental import pallas as pl
from jax.experimental.pallas import tpu as pltpu
from jax.sharding import PartitionSpec as P

XM = 128
ALIGN = 16
OUT_CHUNKS = 8
GROUP = 4
TABLE_LIMIT = 16 * 2**20
VMEM_LIMIT = 40 * 2**20
MESH = pl.DeviceIdType.MESH
F32 = jnp.float32
BF16 = jnp.bfloat16


def dft(length, sign, scaling):
    ids = np.arange(length)
    angles = 2.0 * np.pi / length * (ids[:, None] * ids[None, :] % length)
    return np.cos(angles) * scaling, sign * np.sin(angles) * scaling


def stacked(real_part, imag_part, axis):
    return np.concatenate([real_part, imag_part], axis=axis).astype(jnp.bfloat16)


def window_tables(length):
    taper = 0.3 + 0.7 * np.sin(np.pi * (np.arange(length) + 0.5) / length) ** 2
    scaling = 1.0 / math.sqrt(length)
    fwd_re, fwd_im = dft(length, -1.0, scaling)
    back_re, back_im = dft(length, 1.0, scaling)
    forward = stacked(fwd_re * taper[None, :], fwd_im * taper[None, :], 0)
    backward = stacked(back_re * taper[:, None], back_im * taper[:, None], 1)
    return forward, backward


def mm(a, b):
    return jnp.dot(a, b, preferred_element_type=F32)


def iota(shape, dim):
    return lax.broadcasted_iota(jnp.int32, shape, dim)


def one_hot(hit):
    return jnp.where(hit, 1.0, 0.0).astype(BF16)


def exchange_kernel(
    nf, ncol, near, early, folded, starts_in, fac_in, prep, wts, fwd_in, bwd_in, win_in, fmap, qtab,
    terms, values, maps, starts_out,
    starts, fac, fwd, bwd, win, pv, qv, wv, send1, recv1, acc, send2, places, shifts, ctab, svec, sall, fv, wdup,
    ld, s1, r1, s2, sd, sx, sp, ro_near, ro_far, rx_near, rx_far, rp, ss, rs,
):
    me = lax.axis_index("facet")
    c = lax.axis_index("col")
    nx = ncol // 2
    xq, core = lax.div(c, 2), lax.rem(c, 2)
    partner = xq * 2 + 1 - core
    pow2 = nf & (nf - 1) == 0
    blocks = prep.shape[1]
    xa, width = wts.shape[1:]
    half = width // 2
    oc = fmap.shape[0]
    deep = nf <= 8
    middle = (near + nf) // 2

    bits = [1 << b for b in range((nf - 1).bit_length())] if pow2 else []
    flips = [b - 2 * b * lax.rem(lax.div(me, b), 2) for b in bits]
    across = [lax.rem(xq + q, nx) * 2 + core for q in range(nx)]
    behind = [lax.rem(xq + nx - q, nx) * 2 + core for q in range(nx)]

    def peer(i):
        if not pow2:
            return lax.rem(me + i, nf)
        out = me
        for b, flip in zip(bits, flips):
            if isinstance(i, int):
                out = out + flip if i & b else out
            else:
                out = out + flip * lax.rem(lax.div(i, b), 2)
        return out

    def source(i):
        return peer(i) if pow2 else lax.rem(me + nf - i, nf)

    def each(first, last, step):
        if not deep:
            pl.loop(first, last)(step)
            return
        for i in range(first, last):
            step(i)

    def each_down(first, last, step):
        each(0, last - first, lambda k: step(last - 1 - k))

    barrier = pltpu.get_barrier_semaphore()

    def greet(i):
        pl.semaphore_signal(barrier, inc=1, device_id={"facet": peer(i)}, device_id_type=MESH)

    each(1, nf, greet)

    for i in range(1, ncol):
        pl.semaphore_signal(
            barrier, inc=1, device_id={"col": lax.rem(c + i, ncol)}, device_id_type=MESH
        )

    def greet_across(i):
        for q in range(1, nx):
            pl.semaphore_signal(
                barrier, inc=1, device_id={"facet": peer(i), "col": across[q]}, device_id_type=MESH
            )

    each(1, near, greet_across)

    strip_load = pltpu.make_async_copy(prep, pv, ld.at[0])
    small = [(starts_in, starts), (fac_in, fac), (fwd_in, fwd)]
    later = [(win_in, win), (fmap, fv), (bwd_in, bwd), (wts, wv), (qtab, qv)]
    small = [pltpu.make_async_copy(*pair, ld.at[1 + k]) for k, pair in enumerate(small)]
    later = [pltpu.make_async_copy(*pair, ld.at[4 + k]) for k, pair in enumerate(later)]
    for copy in [*small, strip_load, *later]:
        copy.start()
    win_load, f_load, b_load, w_load, q_load = later
    for copy in small:
        copy.wait()

    lane = iota(svec.shape, 1)
    row = jnp.zeros(svec.shape, jnp.int32)
    svec[...] = lax.fori_loop(0, nf, lambda j, v: jnp.where(lane == j, starts[j], v), row)

    def remote(src, dst, send, recv, **where):
        return pltpu.make_async_remote_copy(
            src_ref=src, dst_ref=dst, send_sem=send, recv_sem=recv,
            device_id=where, device_id_type=MESH,
        )

    def send_first(h, i, far):
        j = peer(i)
        return remote(send1.at[h, j], recv1.at[h, i], s1.at[h], r1.at[h, far], facet=j)

    def own_arrival(h, i, far):
        return ro_far.at[h, i - near] if far else ro_near.at[h]

    def across_arrival(h, i, q, far):
        return rx_far.at[q - 1, h, i - near] if far else rx_near.at[q - 1, h]

    def send_second(h, i, far):
        j = peer(i)
        arrived = own_arrival(h, i, far)
        return remote(send2.at[h, j], terms.at[c, me, h], s2.at[h], arrived, facet=j)

    def send_direct(h, i, q):
        j = peer(i)
        return remote(
            send2.at[h, j], terms.at[c, me, h], sd.at[q - 1, h], across_arrival(h, i, q, 0),
            facet=j, col=across[q],
        )

    def forward_x(h, i, q, far):
        block = terms.at[c, source(i), h]
        arrived = across_arrival(h, i, q, far)
        return remote(block, block, sx.at[q - 1, h], arrived, col=across[q])

    def forward_partner(cc, h, i, far):
        block = terms.at[cc, source(i), h]
        return remote(block, block, sp.at[h], rp.at[far * (1 + h)], col=partner)

    def sent(block, sem):
        remote(block, block, sem, rs.at[0], col=partner).wait_send()

    def received(block, sem):
        remote(block, block, ss.at[0], sem, col=partner).wait_recv()

    row_d = iota((XM, 2 * XM), 1) - iota((XM, 2 * XM), 0)
    fwd_table = fwd[...]

    def contribution(j, dst, at):
        start = starts[j]
        block = lax.div(start, XM)
        shift = start - block * XM
        above = jnp.where(block + 1 == blocks, 0, block + 1)
        top = jnp.concatenate([pv[0, block], pv[1, block]], axis=1)
        low = jnp.concatenate([pv[0, above], pv[1, above]], axis=1)
        picked = mm(one_hot(row_d == shift), jnp.concatenate([top, low], axis=0))
        prod = mm(fwd_table, picked.astype(BF16))
        re = prod[:XM, :width] - prod[XM:, width:]
        im = prod[:XM, width:] + prod[XM:, :width]
        first = iota(re.shape, 1) < half
        dst[0, at] = jnp.where(first, re, pltpu.roll(im, half, 1)).astype(BF16)
        dst[1, at] = jnp.where(first, pltpu.roll(re, half, 1), im).astype(BF16)

    def window_maps():
        win_load.wait()
        f_load.wait()
        fm = fv[...]
        col_n = iota((oc, width), 0)
        for k in range(ncol):
            m = lax.dot_general(
                one_hot(col_n == win[k : k + 1, :]), fm, (((0,), (0,)), ((), ())),
                preferred_element_type=F32,
            ).astype(BF16)
            m_re, m_im = m[:, :oc], m[:, oc:]
            upper = jnp.concatenate([m_re, m_im], axis=1)
            lower = jnp.concatenate([-m_im, m_re], axis=1)
            maps[k] = jnp.concatenate(
                [upper[:half], lower[:half], upper[half:], lower[half:]], axis=0
            )

    strip_load.wait()
    pl.semaphore_wait(barrier, nf - 1 + ncol - 1 + (near - 1) * (nx - 1))

    def first(i, far):
        contribution(peer(i), send1, peer(i))
        send_first(0, i, far).start()

    each_down(near, nf, lambda i: first(i, 1))
    each_down(1, near, lambda i: first(i, 0))

    contribution(me, recv1, 0)

    for i in range(1, ncol):
        to = lax.rem(c + i, ncol)
        remote(svec, sall.at[c], ss.at[0], rs.at[0], col=to).start()
    sall[c] = svec[...]

    grid_d = iota((xa, XM), 0) - iota((xa, XM), 1)
    back_d = iota((XM, xa), 1) - iota((XM, xa), 0)

    def hit(diff, j):
        return one_hot((diff == fac[j]) | (diff == fac[j] - xa))

    if folded:
        for i in range(nf):
            places[:, i * XM : (i + 1) * XM] = hit(grid_d, source(i))

    w_load.wait()
    near_lane = iota((xa, width), 1) < half
    for p in range(2):
        w = wv[p].astype(F32)
        swapped = pltpu.roll(w, half, 1)
        wdup[0, p] = jnp.where(near_lane, w, swapped)
        wdup[1, p] = jnp.where(near_lane, swapped, w)

    b_load.wait()
    turn_d = iota((XM, XM), 0) - iota((XM, XM), 1)
    turn_by = lax.rem(starts[me], ALIGN)
    turn = (turn_d == turn_by) | (turn_d == turn_by - XM)
    turned = mm(one_hot(turn), bwd[...]).astype(BF16)
    turned = jnp.concatenate([turned[:, :XM], turned[:, XM:]], axis=0)

    q_load.wait()
    column = iota((nf, xa), 0)
    at_row = jnp.zeros((nf, xa), jnp.int32)
    at_row = lax.fori_loop(0, nf, lambda j, v: jnp.where(column == j, fac[j], v), at_row)
    picks = one_hot(iota((nf, xa), 1) == at_row)
    unit = math.sqrt(nf * XM) * image_gain(nf, xa)
    shifts[0] = mm(picks, qv[:xa]) * unit
    shifts[1] = mm(picks, qv[xa:]) * -unit
    with_re = mm(turned, qv[:XM])
    with_im = mm(turned, qv[xa : xa + XM])
    base_re = with_re[:XM] + with_im[XM:]
    base_im = with_re[XM:] - with_im[:XM]

    def back_table(j):
        re, im = shifts[0, pl.ds(j, 1), :], shifts[1, pl.ds(j, 1), :]
        ctab[j, :XM] = (base_re * re - base_im * im).astype(BF16)
        ctab[j, XM:] = (base_re * im + base_im * re).astype(BF16)

    each(0, nf, back_table)

    sent(send1.at[0, pl.ds(0, nf - 1)], s1.at[0])
    each_down(near, nf, lambda i: send_first(1, i, 1).start())
    each_down(1, near, lambda i: send_first(1, i, 0).start())

    def twist(prod):
        n = prod.shape[0] // 2
        crossed = pltpu.roll(prod[n:], half, 1)
        first = iota(crossed.shape, 1) < half
        return prod[:n] + jnp.where(first, -crossed, crossed)

    def arrived(h, first, last):
        return recv1[h, first:last].reshape((last - first) * XM, width)

    for h in range(2):
        near_blocks, far_blocks = recv1.at[h, pl.ds(0, near - 1)], recv1.at[h, pl.ds(0, nf - near)]
        if folded:
            split = near * XM
            received(near_blocks, r1.at[h, 0])
            acc[...] = mm(places[:, :split], arrived(h, 0, near))
            received(far_blocks, r1.at[h, 1])
            acc[...] += mm(places[:, split:], arrived(h, near, nf))
        else:
            acc[...] = mm(hit(grid_d, me), recv1[h, 0])

            def gather(i):
                acc[...] += mm(hit(grid_d, source(i)), recv1[h, i])

            received(near_blocks, r1.at[h, 0])
            each(1, near, gather)
            received(far_blocks, r1.at[h, 1])
            each(near, nf, gather)
        prod = mm(qv[...], acc[...].astype(BF16))
        spectrum = twist(prod)
        crossed = wdup[h, 1] * pltpu.roll(spectrum, half, 1)
        weighted = wdup[h, 0] * spectrum + jnp.where(near_lane, -crossed, crossed)
        weighted = weighted.astype(BF16)

        def back(j):
            return twist(mm(ctab[j], weighted)).astype(BF16)

        terms[c, me, h] = back(me)
        for q in range(1, nx):
            forward_x(h, 0, q, 0).start()
        forward_partner(c, h, 0, 0).start()

        def second(i, far, late=False):
            j = peer(i)
            send2[h, j] = back(j)
            if not (h and late):
                send_second(h, i, far).start()

        def second_near(i):
            second(i, 0)
            for q in range(1, nx):
                send_direct(h, i, q).start()

        each(1, near, second_near)
        each(near, middle, lambda i: second(i, 1))
        each(middle, nf, lambda i: second(i, 1, True))
        if h == 0:
            window_maps()

    sent(sall.at[pl.ds(0, ncol - 1)], ss.at[0])
    received(sall.at[pl.ds(0, ncol - 1)], rs.at[0])
    starts_copy = pltpu.make_async_copy(sall, starts_out, ld.at[9])
    starts_copy.start()

    def relay_near(h):
        received(terms.at[0, pl.ds(0, near - 1), h], ro_near.at[h])
        each(1, near, lambda i: forward_partner(c, h, i, 0).start())

    def relay_across_near(h):
        for q in range(1, nx):
            received(terms.at[0, pl.ds(0, near), h], rx_near.at[q - 1, h])
            each(0, near, lambda i: forward_partner(behind[q], h, i, 0).start())

    def relay_far(i, h):
        received(terms.at[c, source(i), h], own_arrival(h, i, 1))
        for q in range(1, nx):
            forward_x(h, i, q, 1).start()
        forward_partner(c, h, i, 1).start()

    def relay_across(i, h):
        for q in range(1, nx):
            received(terms.at[behind[q], source(i), h], across_arrival(h, i, q, 1))
            forward_partner(behind[q], h, i, 1).start()

    def relay_both(i):
        relay_far(i, 1)
        relay_across(i, 0)

    def map_near(i):
        j = source(i)
        for k in range(ncol):
            values[k, i] = mm(jnp.concatenate([terms[k, j, 0], terms[k, j, 1]], axis=1), maps[k])

    each(near, near + 1, lambda i: relay_far(i, 0))
    each(middle, nf, lambda i: send_second(1, i, 1).start())
    each(near + 1, nf, lambda i: relay_far(i, 0))
    relay_near(0)
    relay_near(1)
    relay_across_near(0)
    relay_across_near(1)
    received(terms.at[pl.ds(0, nx), pl.ds(0, near)], rp.at[0])
    def relay_map(i):
        relay_both(i)
        if early:
            map_near(i - near)

    each(near, nf, relay_map)
    each(near, nf, lambda i: relay_across(i, 1))
    for h in range(2):
        received(terms.at[pl.ds(0, nx), pl.ds(0, nf - near), h], rp.at[1 + h])

    starts_copy.wait()
    for h in range(2):
        if h:
            sent(send1.at[h, pl.ds(0, nf - 1)], s1.at[h])
        sent(send2.at[h, pl.ds(0, nf - 1)], s2.at[h])
        sent(terms.at[pl.ds(0, nx), :, h], sp.at[h])
        for q in range(1, nx):
            sent(terms.at[0, pl.ds(0, near - 1), h], sd.at[q - 1, h])
            sent(terms.at[0, pl.ds(0, nf - near + 1), h], sx.at[q - 1, h])


def image_gain(nf, xa):
    return math.sqrt(nf * XM) / math.sqrt(xa)


def finish_kernel(nf, ncol, near, early, starts_all, terms, values, maps, out, acc, stage, seen, code, osem):
    me = lax.axis_index("facet")
    c = lax.axis_index("col")
    own_rows = out.shape[1]
    oc = out.shape[2]
    total = own_rows * ncol
    base = c * own_rows
    pow2 = nf & (nf - 1) == 0

    def source(i):
        if not pow2:
            return lax.rem(me + nf - i, nf)
        return jnp.bitwise_xor(me, i)

    acc[...] = jnp.zeros_like(acc)
    slot = iota((XM, 2 * oc), 0)
    edge = iota((ALIGN, 2 * oc), 0)

    split = near if early else 0
    mid = XM + own_rows // 2

    def listed(kind, first, last):
        def note(cc, i, counts):
            upper, lower = counts
            j = source(i)
            rel = starts_all[cc, 0, j] - base
            rel = jnp.where(rel < 0, rel + total, rel)
            rel = jnp.where(rel >= total - XM, rel - total, rel) + XM
            inside = rel < own_rows + XM
            is_lower = rel >= mid
            spot = jnp.where(is_lower, lower, upper)
            place = jnp.where(is_lower, 1, 0)
            seen[kind, place, spot] = rel
            code[kind, place, spot] = i * ncol + cc
            one = jnp.where(inside, 1, 0)
            return upper + one * (1 - place), lower + one * place

        zero = jnp.int32(0)
        counts = (zero, zero)
        for cc in range(ncol):
            if nf <= 8:
                for i in range(first, last):
                    counts = note(cc, i, counts)
            else:
                counts = lax.fori_loop(first, last, lambda i, n: note(cc, i, n), counts)
        for place in range(2):
            for k in range(GROUP - 1):
                seen[kind, place, counts[place] + k] = 0
                code[kind, place, counts[place] + k] = first * ncol
        return counts

    def gather(kind, place, count, value_of):
        def load(t):
            term = code[kind, place, t]
            i = lax.div(term, ncol)
            return seen[kind, place, t], value_of(term - i * ncol, i, source(i))

        def add(rel, value):
            turn = jnp.bitwise_and(rel, ALIGN - 1)
            low = pl.multiple_of(rel - turn, ALIGN)
            acc[pl.ds(low, XM), :] += jnp.where(slot >= turn, value, 0.0)
            acc[pl.ds(pl.multiple_of(low + XM, ALIGN), ALIGN), :] += jnp.where(
                edge < turn, value[:ALIGN], 0.0
            )

        @pl.loop(0, lax.div(count + GROUP - 1, GROUP))
        def _(t):
            pairs = [load(t * GROUP + k) for k in range(GROUP)]
            for rel, value in pairs:
                add(rel, value)

    def mapped(cc, i, j):
        return mm(jnp.concatenate([terms[cc, j, 0], terms[cc, j, 1]], axis=1), maps[cc])

    early_counts = listed(0, 0, split) if early else None
    late_counts = listed(1, split, nf)
    chunk = own_rows // OUT_CHUNKS
    for place in range(2):
        if early:
            gather(0, place, early_counts[place], lambda cc, i, j: values[cc, i])
        gather(1, place, late_counts[place], mapped)
        for k in range(place * OUT_CHUNKS // 2, (place + 1) * OUT_CHUNKS // 2):
            rows = pl.ds(k * chunk, chunk)
            src = pl.ds(XM + k * chunk, chunk)
            stage[0, rows, :] = acc[src, :oc].astype(BF16)
            stage[1, rows, :] = acc[src, oc:].astype(BF16)
            pltpu.make_async_copy(stage.at[:, rows, :], out.at[:, rows, :], osem.at[0]).start()
    pltpu.make_async_copy(stage, out, osem.at[0]).wait()


def body(prepared, sub_off, fac_off, win_col, vis_weights):
    nf = fac_off.shape[0]
    ncol = lax.axis_size("col")
    facet_strip = prepared[0]
    facet_len, width = facet_strip.shape[1:]
    strip_blocks = facet_strip.reshape(2, facet_len // XM, XM, width)
    weights = vis_weights[0]
    xa = weights.shape[1]
    oc = width * ncol // 2
    own_rows = facet_len // ncol
    starts = sub_off[:, 0]
    lanes = -(-nf // 128) * 128
    near = nf // 2 if nf & (nf - 1) == 0 else 1
    nx = ncol // 2
    early = ncol * near * XM * 2 * oc * 4 <= TABLE_LIMIT
    folded = xa * nf * XM * 2 <= TABLE_LIMIT // 4

    forward, backward = window_tables(XM)
    q_table = stacked(*dft(xa, -1.0, 1.0 / math.sqrt(nf * XM)), 0)
    out_map = stacked(*dft(oc, 1.0, 1.0 / math.sqrt(2 * oc)), 1)

    smem = pl.BlockSpec(memory_space=pltpu.SMEM)
    vmem = pl.BlockSpec(memory_space=pltpu.VMEM)
    hbm = pl.BlockSpec(memory_space=pl.ANY)
    dma = pltpu.SemaphoreType.DMA
    halves = pltpu.VMEM((2, nf, XM, width), BF16)
    operands = (
        starts, fac_off, strip_blocks, weights, jnp.asarray(forward), jnp.asarray(backward),
        win_col, jnp.asarray(out_map), jnp.asarray(q_table),
    )
    held = (ncol, near, XM, 2 * oc) if early else (8, 128)
    results = pl.pallas_call(
        functools.partial(exchange_kernel, nf, ncol, near, early, folded),
        out_shape=(
            pltpu.VMEM((ncol, nf, 2, XM, width), BF16),
            pltpu.VMEM(held, F32),
            pltpu.VMEM((ncol, 2 * width, 2 * oc), BF16),
            pltpu.SMEM((ncol, 8, lanes), jnp.int32),
        ),
        in_specs=[hbm] * len(operands),
        out_specs=(vmem, vmem, vmem, smem),
        scratch_shapes=[
            pltpu.SMEM((nf,), jnp.int32),
            pltpu.SMEM((nf,), jnp.int32),
            pltpu.VMEM(forward.shape, BF16),
            pltpu.VMEM(backward.shape, BF16),
            pltpu.VMEM(win_col.shape, jnp.int32),
            pltpu.VMEM(strip_blocks.shape, BF16),
            pltpu.VMEM(q_table.shape, BF16),
            pltpu.VMEM(weights.shape, BF16),
            halves,
            halves,
            pltpu.VMEM((xa, width), F32),
            halves,
            pltpu.VMEM((xa, nf * XM) if folded else (8, 128), BF16),
            pltpu.VMEM((2, nf, xa), F32),
            pltpu.VMEM((nf, 2 * XM, xa), BF16),
            pltpu.VMEM((8, lanes), jnp.int32),
            pltpu.VMEM((ncol, 8, lanes), jnp.int32),
            pltpu.VMEM(out_map.shape, BF16),
            pltpu.VMEM((2, 2, xa, width), F32),
            dma((10,)), dma((2,)), dma((2, 2)), dma((2,)),
            dma((nx - 1, 2)), dma((nx - 1, 2)), dma((2,)),
            dma((2,)), dma((2, nf - near)), dma((nx - 1, 2)), dma((nx - 1, 2, nf - near)), dma((3,)),
            dma((1,)), dma((1,)),
        ],
        compiler_params=pltpu.CompilerParams(
            collective_id=0, has_side_effects=True, vmem_limit_bytes=VMEM_LIMIT
        ),
        name="exchange",
    )(*[pltpu.with_memory_space_constraint(x, pltpu.HBM) for x in operands])
    terms, values, maps, starts_all = results
    spaces = (pltpu.SMEM, pltpu.VMEM, pltpu.VMEM, pltpu.VMEM)
    out = pl.pallas_call(
        functools.partial(finish_kernel, nf, ncol, near, early),
        out_shape=jax.ShapeDtypeStruct((2, own_rows, oc), BF16),
        in_specs=[smem, vmem, vmem, vmem],
        out_specs=hbm,
        scratch_shapes=[
            pltpu.VMEM((own_rows + 2 * XM + ALIGN, 2 * oc), F32),
            pltpu.VMEM((2, own_rows, oc), BF16),
            pltpu.SMEM((2, 2, ncol * nf + GROUP), jnp.int32),
            pltpu.SMEM((2, 2, ncol * nf + GROUP), jnp.int32),
            dma((1,)),
        ],
        compiler_params=pltpu.CompilerParams(vmem_limit_bytes=VMEM_LIMIT),
        name="finish",
    )(*[pltpu.with_memory_space_constraint(x, m) for x, m in zip((starts_all, terms, values, maps), spaces)])
    return out[None]


def solution(mesh):
    in_specs = (
        P("facet", None, None, "col"),
        P(None, "col"),
        P(),
        P(),
        P("facet", None, None, "col"),
    )
    out_specs = P("facet", None, "col", None)
    return jax.shard_map(body, mesh=mesh, in_specs=in_specs, out_specs=out_specs, check_vma=False)
```
